32 devices in a mesh: ctx: 8 (over y, x, core), chan: 4 (over z).
Axes of the slice: x: 2, y: 2, z: 4, core: 2. Of those that a mesh axis runs over, the one named last changes fastest.
Arguments:
- queries: bfloat16 [1024, 4096], P('ctx', 'chan'), may hold values from -8 to 8
- key_rows: bfloat16 [1024, 4096], P('ctx', 'chan'), may hold values from -8 to 8
- value_rows: bfloat16 [1024, 4096], P('ctx', 'chan'), may hold values from -16 to 16
- gate_in: bfloat16 [1024, 4096], P('ctx', 'chan'), may hold values from -6 to 6
- gate_out: bfloat16 [1024, 4096], P('ctx', 'chan'), may hold values from -6 to 6
- kernel_taps: float32 [512, 7], P('chan'), may hold values from -2 to 2
- norm_gain: float32 [4096], P('chan'), may hold values from 0.1 to 1.9
- cotangent: bfloat16 [1024, 4096], P('ctx', 'chan'), may hold values from -6 to 6
Outputs:
- mixed: bfloat16 [1024, 4096], P('ctx', 'chan')
- grad_queries: bfloat16 [1024, 4096], P('ctx', 'chan')
- grad_keys: bfloat16 [1024, 4096], P('ctx', 'chan')
- grad_values: bfloat16 [1024, 4096], P('ctx', 'chan')
- grad_gate_in: bfloat16 [1024, 4096], P('ctx', 'chan')
- grad_gate_out: bfloat16 [1024, 4096], P('ctx', 'chan')
- grad_filter: float32 [512, 7], P('chan')
- grad_gain: float32 [4096], P('chan')
The draws below stay inside these ranges and needn't reach their ends.
All inputs are finite; a program needn't handle non-finite values.
Results may differ from the reference program's by a relative error of at most 0.015.
Values may be sent and summed in bfloat16 or wider, within the bound.
No kernel may reach another device: no remote copies, remote signals or barrier semaphores. Data moves between devices by JAX's collectives and lax.ppermute only.
A program may use at most 128 MiB of HBM per device.

```python
import jax
import jax.numpy as jnp
from jax import lax

HEADS = 32
HEAD = 128
GROUPS = 512
FILT = 7
TOKENS = 1024
WIDTH = 4096
GROUP_SIZE = 8


def draw_queries(key, part):
    shape = (TOKENS, HEADS * HEAD)
    values = jnp.clip(jax.random.normal(jax.random.fold_in(key, 1), shape, jnp.float32), -4.0, 4.0)
    return values.astype(jnp.bfloat16)


def draw_key_rows(key, part):
    shape = (TOKENS, HEADS * HEAD)
    values = jnp.clip(jax.random.normal(jax.random.fold_in(key, 2), shape, jnp.float32), -4.0, 4.0)
    return values.astype(jnp.bfloat16)


def draw_value_rows(key, part):
    shape = (TOKENS, HEADS * HEAD)
    column = jnp.arange(HEADS * HEAD, dtype=jnp.float32) / (HEADS * HEAD)
    spread = jnp.exp(jax.random.uniform(jax.random.fold_in(key, 4), (HEADS * HEAD,), jnp.float32, 0.0, 1.2))
    base = jnp.clip(jax.random.normal(jax.random.fold_in(key, 3), shape, jnp.float32), -4.0, 4.0)
    trend = jnp.exp(1.1 * column)
    return jnp.clip(base * (trend * spread)[None, :], -16.0, 16.0).astype(jnp.bfloat16)


def steps_of(rng, dims, split, smallest, largest):
    def one(axis_at, parts):
        heights = jax.random.uniform(jax.random.fold_in(jax.random.fold_in(rng, 6), axis_at), (parts,), jnp.float32, smallest / len(split), largest / len(split))
        return jnp.repeat(jnp.exp(heights), dims[axis_at] // parts).reshape((-1,) + (1,) * (len(dims) - axis_at - 1))

    loudness = one(*split[0])
    for cut in split[1:]:
        loudness = loudness * one(*cut)
    return loudness


def scatter_about(rng, extent, scale, bound, split=(), kind=jnp.bfloat16):
    values = scale * jax.random.normal(rng, extent, jnp.float32)
    if split:
        values = values * steps_of(rng, extent, split, -0.22, 0.18)
    return jnp.clip(values, -bound, bound).astype(kind)


def setup_inputs(seed: int = 0) -> dict:
    key_list = jax.random.split(jax.random.key(seed), 9)
    queries = draw_queries(jax.random.fold_in(key_list[8], 71), 0)
    key_rows = draw_key_rows(jax.random.fold_in(key_list[8], 71), 0)
    value_rows = draw_value_rows(jax.random.fold_in(key_list[8], 71), 0)
    gate_in = scatter_about(key_list[3], (TOKENS, WIDTH), 1.0, 6.0, ((0, 8), (1, 4)))
    gate_out = scatter_about(key_list[4], (TOKENS, WIDTH), 1.0, 6.0, ((0, 8), (1, 4)))
    kernel_taps = scatter_about(key_list[5], (GROUPS, FILT), 0.4, 2.0, ((0, 4),), jnp.float32)
    norm_gain = jnp.clip(1.0 + 0.18 * jax.random.normal(key_list[6], (WIDTH,), jnp.float32), 0.1, 1.9)
    cotangent = scatter_about(key_list[7], (TOKENS, WIDTH), 1.0, 6.0, ((0, 8), (1, 4)))
    return dict(queries=queries, key_rows=key_rows, value_rows=value_rows, gate_in=gate_in, gate_out=gate_out, kernel_taps=kernel_taps, norm_gain=norm_gain, cotangent=cotangent)


EPS = 1e-06
NEG = -1e+30

def causal_scores(q_head, k_head):
    scores = jnp.dot(q_head, k_head.T, precision=lax.Precision.HIGHEST) * HEAD ** (-0.5)
    rows_pos = jnp.arange(TOKENS, dtype=jnp.int32)
    allowed = rows_pos[:, None] >= rows_pos[None, :]
    return jnp.where(allowed, scores, NEG)

def round_trip(values):
    return lax.optimization_barrier(values.astype(jnp.bfloat16)).astype(jnp.float32)

def head_forward(blocks):
    q_head, k_head, v_head = blocks
    scores = causal_scores(q_head, k_head)
    row_max = lax.optimization_barrier(jnp.max(scores, axis=1, keepdims=True))
    lse = row_max[:, 0] + jnp.log(lax.optimization_barrier(jnp.sum(jnp.exp(scores - row_max), axis=1)))
    weights = round_trip(jnp.exp(scores - lse[:, None]))
    output = jnp.dot(weights, v_head, precision=lax.Precision.HIGHEST)
    return (output.astype(jnp.bfloat16), lse)

def head_backward(blocks):
    q_head, k_head, v_head, lse, d_out, delta = blocks
    scores = causal_scores(q_head, k_head)
    weights = jnp.exp(scores - lse[:, None])
    d_probs = jnp.dot(d_out, v_head.T, precision=lax.Precision.HIGHEST)
    d_scores = round_trip(weights * (d_probs - delta[:, None]))
    scale = HEAD ** (-0.5)
    grad_q = (jnp.dot(d_scores, k_head, precision=lax.Precision.HIGHEST) * scale).astype(jnp.bfloat16)
    grad_k = (jnp.dot(d_scores.T, q_head, precision=lax.Precision.HIGHEST) * scale).astype(jnp.bfloat16)
    grad_v = jnp.dot(round_trip(weights).T, d_out, precision=lax.Precision.HIGHEST).astype(jnp.bfloat16)
    return (grad_q, grad_k, grad_v)

def split_heads(matrix):
    return matrix.astype(jnp.float32).reshape(TOKENS, HEADS, HEAD).transpose(1, 0, 2)

def join_heads(stacked):
    return stacked.transpose(1, 0, 2).reshape(TOKENS, WIDTH)

def shift_down(field, lag):
    return jnp.pad(field, ((lag, 0), (0, 0)))[:TOKENS]

def shift_up(field, lag):
    return jnp.pad(field, ((0, lag), (0, 0)))[lag:]

def reference(queries, key_rows, value_rows, gate_in, gate_out, kernel_taps, norm_gain, cotangent):
    q_heads = split_heads(queries)
    k_heads = split_heads(key_rows)
    v_heads = split_heads(value_rows)
    out_heads, lse_heads = lax.map(head_forward, (q_heads, k_heads, v_heads))
    attn = join_heads(out_heads)
    attn_wide = attn.astype(jnp.float32)
    rstd = 1.0 / jnp.sqrt(lax.optimization_barrier(jnp.sum(attn_wide * attn_wide, axis=1)) / WIDTH + EPS)
    normed = attn_wide * rstd[:, None] * norm_gain[None, :]
    gate_wide = gate_in.astype(jnp.float32)
    mixed_in = gate_wide * normed
    taps = jnp.repeat(kernel_taps, GROUP_SIZE, axis=0)
    conv_out = jnp.zeros((TOKENS, WIDTH), jnp.float32)
    for lag in range(FILT):
        conv_out = conv_out + taps[:, lag][None, :] * shift_down(mixed_in, lag)
    out_gate = gate_out.astype(jnp.float32)
    mixed = (out_gate * conv_out).astype(jnp.bfloat16)
    upstream = cotangent.astype(jnp.float32)
    grad_gate_out = (upstream * conv_out).astype(jnp.bfloat16)
    d_conv = upstream * out_gate
    columns = []
    d_mixed = jnp.zeros((TOKENS, WIDTH), jnp.float32)
    for lag in range(FILT):
        per_channel = lax.optimization_barrier(jnp.sum(d_conv * shift_down(mixed_in, lag), axis=0))
        columns.append(per_channel.reshape(GROUPS, GROUP_SIZE).sum(axis=1))
        d_mixed = d_mixed + taps[:, lag][None, :] * shift_up(d_conv, lag)
    grad_filter = jnp.stack(columns, axis=1)
    grad_gate_in = (d_mixed * normed).astype(jnp.bfloat16)
    d_normed = d_mixed * gate_wide
    grad_gain = lax.optimization_barrier(jnp.sum(d_normed * attn_wide * rstd[:, None], axis=0))
    scaled = d_normed * norm_gain[None, :]
    rowdot = lax.optimization_barrier(jnp.sum(scaled * attn_wide, axis=1))
    d_attn = (rstd[:, None] * scaled - attn_wide * (rstd ** 3 * rowdot / WIDTH)[:, None]).astype(jnp.bfloat16)
    d_heads = split_heads(d_attn)
    delta = lax.optimization_barrier(jnp.sum(d_heads * split_heads(attn), axis=2))
    grad_q, grad_k, grad_v = lax.map(head_backward, (q_heads, k_heads, v_heads, lse_heads, d_heads, delta))
    return (mixed, join_heads(grad_q), join_heads(grad_k), join_heads(grad_v), grad_gate_in, grad_gate_out, grad_filter, grad_gain)
```

```python
import functools

import jax
import jax.numpy as jnp
from jax import lax
from jax.experimental import pallas as pl
from jax.experimental.pallas import tpu as pltpu
from jax.sharding import PartitionSpec as P

HEAD = 128
FILT = 7
WIDTH = 4096


EPS = 1e-06
NEG = -1e30


def from_behind(shard, axis, by):
    length = lax.axis_size(axis)
    pairs = [(i, i + by) for i in range(length) if 0 <= i + by < length]
    return lax.ppermute(shard, axis, pairs)


def score_block(query_heads, key_block, query_pos, key_pos):
    scores = jnp.einsum(
        "rhe,khe->hrk", query_heads, key_block, preferred_element_type=jnp.float32
    ) * HEAD ** (-0.5)
    allowed = query_pos[:, None] >= key_pos[None, :]
    return jnp.where(allowed[None], scores, NEG)


def row_totals(query_heads, query_pos, block_count, keys_heads, block_rows):
    row_count = query_heads.shape[0]
    head_count = query_heads.shape[1]

    def advance(block_index, running):
        row_max, row_sum = running
        first_key = block_index * block_rows
        key_block = lax.dynamic_slice_in_dim(keys_heads, first_key, block_rows, 0)
        key_pos = first_key + jnp.arange(block_rows, dtype=jnp.int32)
        scores = score_block(query_heads, key_block, query_pos, key_pos)
        new_max = jnp.maximum(row_max, jnp.max(scores, axis=2))
        row_sum = row_sum * jnp.exp(row_max - new_max) + jnp.sum(
            jnp.exp(scores - new_max[:, :, None]), axis=2
        )
        return (new_max, row_sum)

    initial = (
        jnp.full((head_count, row_count), NEG, jnp.float32),
        jnp.zeros((head_count, row_count), jnp.float32),
    )
    row_max, row_sum = lax.fori_loop(0, block_count, advance, initial)
    return row_max + jnp.log(row_sum)


def row_outputs(query_heads, query_pos, block_count, keys_heads, values_heads, lse, block_rows):
    row_count = query_heads.shape[0]
    head_count = query_heads.shape[1]

    def advance(block_index, summed):
        first_key = block_index * block_rows
        key_block = lax.dynamic_slice_in_dim(keys_heads, first_key, block_rows, 0)
        value_block = lax.dynamic_slice_in_dim(values_heads, first_key, block_rows, 0)
        key_pos = first_key + jnp.arange(block_rows, dtype=jnp.int32)
        scores = score_block(query_heads, key_block, query_pos, key_pos)
        weights_low = jnp.exp(scores - lse[:, :, None]).astype(jnp.bfloat16)
        return summed + jnp.einsum(
            "hrk,khe->rhe", weights_low, value_block, preferred_element_type=jnp.float32
        )

    summed = lax.fori_loop(
        0, block_count, advance, jnp.zeros((row_count, head_count, HEAD), jnp.float32)
    )
    return summed.reshape(row_count, head_count * HEAD).astype(jnp.bfloat16)


def query_grads(
    query_heads, d_heads, query_pos, block_count, keys_heads, values_heads, lse, delta, block_rows
):
    row_count = query_heads.shape[0]
    head_count = query_heads.shape[1]

    def advance(block_index, summed):
        first_key = block_index * block_rows
        key_block = lax.dynamic_slice_in_dim(keys_heads, first_key, block_rows, 0)
        value_block = lax.dynamic_slice_in_dim(values_heads, first_key, block_rows, 0)
        key_pos = first_key + jnp.arange(block_rows, dtype=jnp.int32)
        scores = score_block(query_heads, key_block, query_pos, key_pos)
        weights = jnp.exp(scores - lse[:, :, None])
        d_probs = jnp.einsum(
            "rhe,khe->hrk", d_heads, value_block, preferred_element_type=jnp.float32
        )
        d_scores = (weights * (d_probs - delta[:, :, None])).astype(jnp.bfloat16)
        return summed + jnp.einsum(
            "hrk,khe->rhe", d_scores, key_block, preferred_element_type=jnp.float32
        )

    summed = lax.fori_loop(
        0, block_count, advance, jnp.zeros((row_count, head_count, HEAD), jnp.float32)
    )
    return (summed * HEAD ** (-0.5)).reshape(row_count, head_count * HEAD).astype(jnp.bfloat16)


def shards_by_rows(queries, key_rows, value_rows, gate_in, gate_out, kernel_taps, norm_gain, cotangent):
    row_count = queries.shape[0]
    channels = queries.shape[1]
    head_count = channels // HEAD
    group_count = kernel_taps.shape[0]
    devices = lax.axis_size("ctx")
    position = lax.axis_index("ctx")
    own_first = position * row_count
    total_rows = row_count * devices
    block_rows = min(512, total_rows)
    local_pos = jnp.arange(row_count, dtype=jnp.int32)
    keys_all, values_all = (
        lax.all_gather(key_rows, "ctx", axis=0, tiled=True),
        lax.all_gather(value_rows, "ctx", axis=0, tiled=True),
    )
    keys_heads = keys_all.reshape(total_rows, head_count, HEAD)
    query_sets = (queries, own_first + local_pos)
    query_block, query_pos = query_sets
    block_count = query_pos[-1] // block_rows + 1
    lse_sets = row_totals(
        query_block.reshape(-1, head_count, HEAD), query_pos, block_count, keys_heads, block_rows
    )
    values_heads = values_all.reshape(total_rows, head_count, HEAD)
    query_block, query_pos = query_sets
    outputs = row_outputs(
        query_block.reshape(-1, head_count, HEAD),
        query_pos,
        block_count,
        keys_heads,
        values_heads,
        lse_sets,
        block_rows,
    )
    lse_rows = lse_sets.T
    attn_wide = outputs.astype(jnp.float32)
    square_sum = lax.psum(jnp.sum(attn_wide * attn_wide, axis=1), "chan")
    inverse_rms = 1.0 / jnp.sqrt(square_sum / WIDTH + EPS)
    normed = attn_wide * inverse_rms[:, None] * norm_gain[None, :]
    gate_wide = gate_in.astype(jnp.float32)
    mixed_in = gate_wide * normed
    taps = jnp.broadcast_to(
        kernel_taps[:, None, :], (group_count, channels // group_count, FILT)
    ).reshape(channels, FILT)
    rim_before = from_behind(mixed_in[row_count - (FILT - 1) :], "ctx", 1)
    extended = jnp.concatenate([rim_before, mixed_in], axis=0)
    conv_out = jnp.zeros((row_count, channels), jnp.float32)
    for lag in range(FILT):
        conv_out = (
            conv_out + taps[:, lag][None, :] * extended[FILT - 1 - lag : FILT - 1 - lag + row_count]
        )
    out_gate = gate_out.astype(jnp.float32)
    mixed = (out_gate * conv_out).astype(jnp.bfloat16)
    upstream = cotangent.astype(jnp.float32)
    grad_gate_out = (upstream * conv_out).astype(jnp.bfloat16)
    d_conv = upstream * out_gate
    tap_columns = []
    for lag in range(FILT):
        per_channel = jnp.sum(
            d_conv * extended[FILT - 1 - lag : FILT - 1 - lag + row_count], axis=0
        )
        tap_columns.append(per_channel.reshape(group_count, -1).sum(axis=1))
    tap_terms = jnp.stack(tap_columns, axis=1)
    rim_after = from_behind(d_conv[: FILT - 1], "ctx", -1)
    extended_grad = jnp.concatenate([d_conv, rim_after], axis=0)
    d_mixed = jnp.zeros((row_count, channels), jnp.float32)
    for lag in range(FILT):
        d_mixed = d_mixed + taps[:, lag][None, :] * extended_grad[lag : lag + row_count]
    grad_gate_in = (d_mixed * normed).astype(jnp.bfloat16)
    d_normed = d_mixed * gate_wide
    gain_terms = jnp.sum(d_normed * attn_wide * inverse_rms[:, None], axis=0)
    grad_filter, grad_gain = lax.psum((tap_terms, gain_terms), "ctx")
    scaled = d_normed * norm_gain[None, :]
    row_dot = lax.psum(jnp.sum(scaled * attn_wide, axis=1), "chan")
    d_attn = (
        inverse_rms[:, None] * scaled - attn_wide * (inverse_rms**3 * row_dot / WIDTH)[:, None]
    ).astype(jnp.bfloat16)
    d_heads = d_attn.reshape(row_count, head_count, HEAD)
    delta_rows = jnp.sum(
        d_heads.astype(jnp.float32) * attn_wide.reshape(row_count, head_count, HEAD), axis=2
    )
    own_count = (own_first + row_count - 1) // block_rows + 1
    grad_queries = query_grads(
        queries.reshape(row_count, head_count, HEAD),
        d_heads,
        own_first + local_pos,
        own_count,
        keys_heads,
        values_heads,
        lse_rows.T,
        delta_rows.T,
        block_rows,
    )
    lse_all, delta_all = (
        lax.all_gather(lse_rows, "ctx", axis=0, tiled=True),
        lax.all_gather(delta_rows, "ctx", axis=0, tiled=True),
    )
    own_keys = key_rows.reshape(row_count, head_count, HEAD)
    own_values = value_rows.reshape(row_count, head_count, HEAD)
    key_pos = own_first + local_pos
    empty_grad = jnp.zeros((row_count, head_count, HEAD), jnp.float32)
    query_piece = lax.all_gather(queries, "ctx", axis=0, tiled=True)
    d_piece = lax.all_gather(d_attn, "ctx", axis=0, tiled=True)
    piece_rows = query_piece.shape[0]

    def contribute(totals):
        query_heads = query_piece.reshape(piece_rows, head_count, HEAD)
        piece_heads = d_piece.reshape(piece_rows, head_count, HEAD)
        query_pos = jnp.arange(piece_rows, dtype=jnp.int32)
        lse_piece = lse_all.T
        delta_piece = delta_all.T
        scores = score_block(query_heads, own_keys, query_pos, key_pos)
        weights = jnp.exp(scores - lse_piece[:, :, None])
        d_probs = jnp.einsum(
            "rhe,khe->hrk", piece_heads, own_values, preferred_element_type=jnp.float32
        )
        d_scores = (weights * (d_probs - delta_piece[:, :, None])).astype(jnp.bfloat16)
        key_grad = jnp.einsum(
            "hrk,rhe->khe", d_scores, query_heads, preferred_element_type=jnp.float32
        )
        value_grad = jnp.einsum(
            "hrk,rhe->khe",
            weights.astype(jnp.bfloat16),
            piece_heads,
            preferred_element_type=jnp.float32,
        )
        return (key_grad, value_grad)

    def unchanged(totals):
        return totals

    key_grad, value_grad = lax.cond(
        jnp.int32(0) + piece_rows > own_first, contribute, unchanged, (empty_grad, empty_grad)
    )
    grad_keys = (key_grad * HEAD ** (-0.5)).reshape(row_count, channels).astype(jnp.bfloat16)
    grad_values = value_grad.reshape(row_count, channels).astype(jnp.bfloat16)
    return (
        mixed,
        grad_queries,
        grad_keys,
        grad_values,
        grad_gate_in,
        grad_gate_out,
        grad_filter,
        grad_gain,
    )


LOG2E = 1.4426950408889634
VMEM_LIMIT = 56 * 1024 * 1024


def vmem_call(body, outs, scratch=(), flops=0, **extra):
    return pl.pallas_call(
        body,
        out_shape=tuple(outs),
        scratch_shapes=list(scratch),
        compiler_params=pltpu.CompilerParams(vmem_limit_bytes=VMEM_LIMIT),
        **extra,
    )


def dot_nt(a, b, precision=None):
    return lax.dot_general(
        a, b, (((1,), (1,)), ((), ())), precision=precision, preferred_element_type=jnp.float32
    )


def dot_nn(a, b):
    return lax.dot_general(a, b, (((1,), (0,)), ((), ())), preferred_element_type=jnp.float32)


def row_sums_as_lanes(product):
    ones = jnp.ones((8, product.shape[1]), jnp.float32)
    return dot_nt(ones, product, lax.Precision.HIGHEST)[0:1]


def channel_taps(taps_ref, head, groups):
    mine = taps_ref[pl.ds(pl.multiple_of(head * groups, 8), groups), :]
    group_of = lax.broadcasted_iota(jnp.int32, (groups, HEAD), 1) // (HEAD // groups)
    spread = (group_of == lax.broadcasted_iota(jnp.int32, (groups, HEAD), 0)).astype(jnp.float32)
    return lax.dot_general(
        mine,
        spread,
        (((0,), (0,)), ((), ())),
        precision=lax.Precision.HIGHEST,
        preferred_element_type=jnp.float32,
    )


def pack_body(q_ref, k_ref, v_ref, gi_ref, go_ref, ct_ref, out_ref):
    rows = q_ref.shape[0]
    for head in range(out_ref.shape[0]):
        cols = slice(head * HEAD, (head + 1) * HEAD)
        for at, ref in enumerate((q_ref, k_ref, v_ref, gi_ref)):
            out_ref[head, at * rows : (at + 1) * rows, :] = ref[:, cols]
        d_conv = go_ref[:, cols].astype(jnp.float32) * ct_ref[:, cols].astype(jnp.float32)
        out_ref[head, 4 * rows : 5 * rows, :] = d_conv.astype(jnp.bfloat16)


def forward_body(axis, rx_ref, taps_ref, gain_ref, p_ref, attn_ref, dz_ref, pay_ref, du_pad, sums):
    blocks = rx_ref.shape[0]
    rows = rx_ref.shape[1] // 5
    tokens = blocks * rows
    wide = 2 * rows if blocks % 2 == 0 else rows
    per = wide // rows
    head = lax.axis_index(axis)
    groups = taps_ref.shape[0] // blocks
    taps = channel_taps(taps_ref, head, groups)
    gain = gain_ref[pl.ds(head, 1), :]

    def part(at, first, count):
        return rx_ref[first : first + count, at * rows : (at + 1) * rows, :].reshape(count * rows, HEAD)

    v_t = part(2, 0, blocks).astype(jnp.float32).T.astype(jnp.bfloat16)
    for b in range(blocks):
        du_pad[b * rows : (b + 1) * rows, :] = part(4, b, 1).astype(jnp.float32)
    du_pad[tokens : tokens + 8, :] = jnp.zeros((8, HEAD), jnp.float32)
    scale = HEAD ** (-0.5) * LOG2E
    for i in range(tokens // wide):
        keys = (i + 1) * wide
        q_i = part(0, i * per, per)
        s = dot_nt(part(1, 0, (i + 1) * per), q_i)
        key_pos = lax.broadcasted_iota(jnp.int32, (wide, wide), 0)
        query_pos = lax.broadcasted_iota(jnp.int32, (wide, wide), 1)
        edge = jnp.where(key_pos <= query_pos, s[keys - wide :], NEG)
        s = edge if i == 0 else jnp.concatenate([s[: keys - wide], edge], axis=0)
        top = jnp.max(s, axis=0, keepdims=True)
        e = jnp.exp2((s - top) * scale)
        p = (e * (1.0 / jnp.sum(e, axis=0, keepdims=True))).astype(jnp.bfloat16)
        p_ref[:keys, i * wide : (i + 1) * wide] = p
        attn_t = dot_nn(v_t[:, :keys], p).astype(jnp.bfloat16).astype(jnp.float32)
        squares = jnp.sum(attn_t * attn_t, axis=0, keepdims=True)
        attn = attn_t.T
        first = i * wide
        attn_ref[first : first + wide, :] = attn.astype(jnp.bfloat16)
        dz = jnp.zeros((wide, HEAD), jnp.float32)
        for lag in range(FILT):
            dz = dz + taps[lag : lag + 1, :] * du_pad[first + lag : first + lag + wide, :]
        dz_ref[first : first + wide, :] = dz
        scaled = dz * part(3, i * per, per).astype(jnp.float32) * gain
        dots = row_sums_as_lanes(scaled * attn)
        for j in range(per):
            at = i * per + j
            sums[at : at + 1, :] = squares[:, j * rows : (j + 1) * rows]
            sums[blocks + at : blocks + at + 1, :] = dots[:, j * rows : (j + 1) * rows]
    low = sums[...].astype(jnp.bfloat16)
    for d in range(pay_ref.shape[0]):
        pay_ref[d] = low


def backward_body(
    axis, width, rs_ref, rx_ref, taps_ref, gain_ref, p_ref, attn_ref, dz_ref, out_ref, z_pad, ds_ref, da_ref, dl_ref
):
    blocks = rx_ref.shape[0]
    rows = rx_ref.shape[1] // 5
    tokens = blocks * rows
    wide = 2 * rows if blocks % 2 == 0 else rows
    per = wide // rows
    head = lax.axis_index(axis)
    groups = taps_ref.shape[0] // blocks
    taps = channel_taps(taps_ref, head, groups)
    gain = gain_ref[pl.ds(head, 1), :]

    def part(at, first, count):
        return rx_ref[first : first + count, at * rows : (at + 1) * rows, :].reshape(count * rows, HEAD)

    totals = jnp.sum(rs_ref[...].astype(jnp.float32), axis=0)
    rstd_lanes = 1.0 / jnp.sqrt(totals[:blocks] / width + EPS)
    pull_lanes = rstd_lanes * rstd_lanes * rstd_lanes * totals[blocks:] / width
    z_pad[0:8, :] = jnp.zeros((8, HEAD), jnp.float32)
    grads = [jnp.zeros((1, HEAD), jnp.float32) for _ in range(FILT + 1)]
    for b in range(blocks):
        first = b * rows
        rstd = jnp.broadcast_to(rstd_lanes[b : b + 1], (HEAD, rows)).T
        pull = jnp.broadcast_to(pull_lanes[b : b + 1], (HEAD, rows)).T
        attn = attn_ref[first : first + rows, :].astype(jnp.float32)
        dz = dz_ref[first : first + rows, :]
        gi = part(3, b, 1).astype(jnp.float32)
        du = part(4, b, 1).astype(jnp.float32)
        normed = attn * rstd * gain
        z_pad[8 + first : 8 + first + rows, :] = gi * normed
        conv = jnp.zeros((rows, HEAD), jnp.float32)
        for lag in range(FILT):
            z = z_pad[8 + first - lag : 8 + first - lag + rows, :]
            conv = conv + taps[lag : lag + 1, :] * z
            grads[lag] = grads[lag] + jnp.sum(du * z, axis=0, keepdims=True)
        d_normed = dz * gi
        grads[FILT] = grads[FILT] + jnp.sum(d_normed * attn * rstd, axis=0, keepdims=True)
        d_attn = (rstd * (d_normed * gain) - attn * pull).astype(jnp.bfloat16)
        da_ref[first : first + rows, :] = d_attn
        dl_ref[0:1, first : first + rows] = row_sums_as_lanes(d_attn.astype(jnp.float32) * attn)
        out_ref[b, 3 * rows : 4 * rows, :] = conv.astype(jnp.bfloat16)
        out_ref[b, 4 * rows : 5 * rows, :] = (dz * normed).astype(jnp.bfloat16)
    both = jnp.concatenate(grads, axis=0)
    high = both.astype(jnp.bfloat16).astype(jnp.float32)
    both = jnp.concatenate([high, both - high], axis=0).astype(jnp.bfloat16)
    for b in range(blocks):
        out_ref[b, 5 * rows : 5 * rows + 16, :] = both
    scale = HEAD ** (-0.5)
    k_t = part(1, 0, blocks).astype(jnp.float32).T.astype(jnp.bfloat16)
    for i in range(tokens // wide):
        first, keys = i * wide, (i + 1) * wide
        dp = dot_nt(part(2, 0, (i + 1) * per), da_ref[first : first + wide, :])
        p = p_ref[:keys, first : first + wide].astype(jnp.float32)
        ds = (p * (dp - dl_ref[0:1, first : first + wide])).astype(jnp.bfloat16)
        ds_ref[:keys, first : first + wide] = ds
        gq = (dot_nn(k_t[:, :keys], ds) * scale).T.astype(jnp.bfloat16)
        for j in range(per):
            out_ref[i * per + j, 0:rows, :] = gq[j * rows : (j + 1) * rows]
    for i in range(tokens // wide):
        first = i * wide
        q = part(0, i * per, blocks - i * per)
        gk = (dot_nn(ds_ref[first : first + wide, first:], q) * scale).astype(jnp.bfloat16)
        gv = dot_nn(p_ref[first : first + wide, first:], da_ref[first:, :]).astype(jnp.bfloat16)
        for j in range(per):
            out_ref[i * per + j, rows : 2 * rows, :] = gk[j * rows : (j + 1) * rows]
            out_ref[i * per + j, 2 * rows : 3 * rows, :] = gv[j * rows : (j + 1) * rows]


def unpack_body(rx_ref, go_ref, ct_ref, mix_ref, gq_ref, gk_ref, gv_ref, ggi_ref, ggo_ref, gf_ref, gg_ref):
    heads = rx_ref.shape[0]
    rows = mix_ref.shape[0]
    groups = gf_ref.shape[0] // heads
    group_of = lax.broadcasted_iota(jnp.int32, (groups, HEAD), 1) // (HEAD // groups)
    gather = (group_of == lax.broadcasted_iota(jnp.int32, (groups, HEAD), 0)).astype(jnp.bfloat16)
    for head in range(heads):
        cols = slice(head * HEAD, (head + 1) * HEAD)
        for at, ref in enumerate((gq_ref, gk_ref, gv_ref)):
            ref[:, cols] = rx_ref[head, at * rows : (at + 1) * rows, :]
        conv = rx_ref[head, 3 * rows : 4 * rows, :].astype(jnp.float32)
        ggi_ref[:, cols] = rx_ref[head, 4 * rows : 5 * rows, :]
        mix_ref[:, cols] = (go_ref[:, cols].astype(jnp.float32) * conv).astype(jnp.bfloat16)
        ggo_ref[:, cols] = (ct_ref[:, cols].astype(jnp.float32) * conv).astype(jnp.bfloat16)
        both = rx_ref[head, 5 * rows : 5 * rows + 16, :]
        sums = dot_nt(gather, both)
        gf_ref[head * groups : (head + 1) * groups, :] = sums[:, :FILT] + sums[:, 8 : 8 + FILT]
        wide = both.astype(jnp.float32)
        gg_ref[head : head + 1, :] = wide[FILT : FILT + 1] + wide[8 + FILT : 8 + FILT + 1]


def shards_by_heads(
    queries, key_rows, value_rows, gate_in, gate_out, kernel_taps, norm_gain, cotangent
):
    rows, channels = queries.shape
    heads = channels // HEAD
    tokens = rows * heads
    everyone = lax.axis_size("ctx") * lax.axis_size("chan")
    low, full = jnp.bfloat16, jnp.float32
    gain = norm_gain.reshape(heads, HEAD)
    (packed,) = vmem_call(pack_body, [jax.ShapeDtypeStruct((heads, 5 * rows, HEAD), low)])(
        queries, key_rows, value_rows, gate_in, gate_out, cotangent
    )
    mine = lax.all_to_all(packed, "ctx", 0, 0, tiled=True)
    probs, attn, d_mixed, partial = vmem_call(
        functools.partial(forward_body, "ctx"),
        [
            jax.ShapeDtypeStruct((tokens, tokens), low),
            jax.ShapeDtypeStruct((tokens, HEAD), low),
            jax.ShapeDtypeStruct((tokens, HEAD), full),
            jax.ShapeDtypeStruct((everyone, 2 * heads, rows), low),
        ],
        [pltpu.VMEM((tokens + 8, HEAD), full), pltpu.VMEM((2 * heads, rows), full)],
    )(mine, kernel_taps, gain)
    sums = lax.all_to_all(partial, ("ctx", "chan"), 0, 0, tiled=True)
    (grads,) = vmem_call(
        functools.partial(backward_body, "ctx", channels * lax.axis_size("chan")),
        [jax.ShapeDtypeStruct((heads, 5 * rows + 16, HEAD), low)],
        [
            pltpu.VMEM((tokens + 8, HEAD), full),
            pltpu.VMEM((tokens, tokens), low),
            pltpu.VMEM((tokens, HEAD), low),
            pltpu.VMEM((8, tokens), full),
        ],
    )(sums, mine, kernel_taps, gain, probs, attn, d_mixed)
    back = lax.all_to_all(grads, "ctx", 0, 0, tiled=True)
    flat = jax.ShapeDtypeStruct((rows, channels), low)
    mixed, gq, gk, gv, ggi, ggo, gf, gg = vmem_call(
        unpack_body,
        [flat] * 6
        + [
            jax.ShapeDtypeStruct(kernel_taps.shape, full),
            jax.ShapeDtypeStruct((heads, HEAD), full),
        ],
    )(back, gate_out, cotangent)
    return (mixed, gq, gk, gv, ggi, ggo, gf, gg.reshape(channels))


def shards(queries, *rest):
    rows, channels = queries.shape
    by_heads = channels // HEAD == lax.axis_size("ctx") and rows == HEAD
    return (shards_by_heads if by_heads else shards_by_rows)(queries, *rest)


def solution(mesh):
    placed = (
        P("ctx", "chan"),
        P("ctx", "chan"),
        P("ctx", "chan"),
        P("ctx", "chan"),
        P("ctx", "chan"),
        P("chan", None),
        P("chan"),
        P("ctx", "chan"),
    )
    return jax.shard_map(
        shards,
        mesh=mesh,
        in_specs=placed,
        out_specs=(
            P("ctx", "chan"),
            P("ctx", "chan"),
            P("ctx", "chan"),
            P("ctx", "chan"),
            P("ctx", "chan"),
            P("ctx", "chan"),
            P("chan", None),
            P("chan"),
        ),
        check_vma=False,
    )
```

```python
import functools

import jax
import jax.numpy as jnp
from jax import lax
from jax.experimental import pallas as pl
from jax.experimental.pallas import tpu as pltpu
from jax.sharding import PartitionSpec as P

HEAD = 128
FILT = 7
WIDTH = 4096


EPS = 1e-06
NEG = -1e30


def from_behind(shard, axis, by):
    length = lax.axis_size(axis)
    pairs = [(i, i + by) for i in range(length) if 0 <= i + by < length]
    return lax.ppermute(shard, axis, pairs)


def score_block(query_heads, key_block, query_pos, key_pos):
    scores = jnp.einsum(
        "rhe,khe->hrk", query_heads, key_block, preferred_element_type=jnp.float32
    ) * HEAD ** (-0.5)
    allowed = query_pos[:, None] >= key_pos[None, :]
    return jnp.where(allowed[None], scores, NEG)


def row_totals(query_heads, query_pos, block_count, keys_heads, block_rows):
    row_count = query_heads.shape[0]
    head_count = query_heads.shape[1]

    def advance(block_index, running):
        row_max, row_sum = running
        first_key = block_index * block_rows
        key_block = lax.dynamic_slice_in_dim(keys_heads, first_key, block_rows, 0)
        key_pos = first_key + jnp.arange(block_rows, dtype=jnp.int32)
        scores = score_block(query_heads, key_block, query_pos, key_pos)
        new_max = jnp.maximum(row_max, jnp.max(scores, axis=2))
        row_sum = row_sum * jnp.exp(row_max - new_max) + jnp.sum(
            jnp.exp(scores - new_max[:, :, None]), axis=2
        )
        return (new_max, row_sum)

    initial = (
        jnp.full((head_count, row_count), NEG, jnp.float32),
        jnp.zeros((head_count, row_count), jnp.float32),
    )
    row_max, row_sum = lax.fori_loop(0, block_count, advance, initial)
    return row_max + jnp.log(row_sum)


def row_outputs(query_heads, query_pos, block_count, keys_heads, values_heads, lse, block_rows):
    row_count = query_heads.shape[0]
    head_count = query_heads.shape[1]

    def advance(block_index, summed):
        first_key = block_index * block_rows
        key_block = lax.dynamic_slice_in_dim(keys_heads, first_key, block_rows, 0)
        value_block = lax.dynamic_slice_in_dim(values_heads, first_key, block_rows, 0)
        key_pos = first_key + jnp.arange(block_rows, dtype=jnp.int32)
        scores = score_block(query_heads, key_block, query_pos, key_pos)
        weights_low = jnp.exp(scores - lse[:, :, None]).astype(jnp.bfloat16)
        return summed + jnp.einsum(
            "hrk,khe->rhe", weights_low, value_block, preferred_element_type=jnp.float32
        )

    summed = lax.fori_loop(
        0, block_count, advance, jnp.zeros((row_count, head_count, HEAD), jnp.float32)
    )
    return summed.reshape(row_count, head_count * HEAD).astype(jnp.bfloat16)


def query_grads(
    query_heads, d_heads, query_pos, block_count, keys_heads, values_heads, lse, delta, block_rows
):
    row_count = query_heads.shape[0]
    head_count = query_heads.shape[1]

    def advance(block_index, summed):
        first_key = block_index * block_rows
        key_block = lax.dynamic_slice_in_dim(keys_heads, first_key, block_rows, 0)
        value_block = lax.dynamic_slice_in_dim(values_heads, first_key, block_rows, 0)
        key_pos = first_key + jnp.arange(block_rows, dtype=jnp.int32)
        scores = score_block(query_heads, key_block, query_pos, key_pos)
        weights = jnp.exp(scores - lse[:, :, None])
        d_probs = jnp.einsum(
            "rhe,khe->hrk", d_heads, value_block, preferred_element_type=jnp.float32
        )
        d_scores = (weights * (d_probs - delta[:, :, None])).astype(jnp.bfloat16)
        return summed + jnp.einsum(
            "hrk,khe->rhe", d_scores, key_block, preferred_element_type=jnp.float32
        )

    summed = lax.fori_loop(
        0, block_count, advance, jnp.zeros((row_count, head_count, HEAD), jnp.float32)
    )
    return (summed * HEAD ** (-0.5)).reshape(row_count, head_count * HEAD).astype(jnp.bfloat16)


def shards_by_rows(queries, key_rows, value_rows, gate_in, gate_out, kernel_taps, norm_gain, cotangent):
    row_count = queries.shape[0]
    channels = queries.shape[1]
    head_count = channels // HEAD
    group_count = kernel_taps.shape[0]
    devices = lax.axis_size("ctx")
    position = lax.axis_index("ctx")
    own_first = position * row_count
    total_rows = row_count * devices
    block_rows = min(512, total_rows)
    local_pos = jnp.arange(row_count, dtype=jnp.int32)
    keys_all, values_all = (
        lax.all_gather(key_rows, "ctx", axis=0, tiled=True),
        lax.all_gather(value_rows, "ctx", axis=0, tiled=True),
    )
    keys_heads = keys_all.reshape(total_rows, head_count, HEAD)
    query_sets = (queries, own_first + local_pos)
    query_block, query_pos = query_sets
    block_count = query_pos[-1] // block_rows + 1
    lse_sets = row_totals(
        query_block.reshape(-1, head_count, HEAD), query_pos, block_count, keys_heads, block_rows
    )
    values_heads = values_all.reshape(total_rows, head_count, HEAD)
    query_block, query_pos = query_sets
    outputs = row_outputs(
        query_block.reshape(-1, head_count, HEAD),
        query_pos,
        block_count,
        keys_heads,
        values_heads,
        lse_sets,
        block_rows,
    )
    lse_rows = lse_sets.T
    attn_wide = outputs.astype(jnp.float32)
    square_sum = lax.psum(jnp.sum(attn_wide * attn_wide, axis=1), "chan")
    inverse_rms = 1.0 / jnp.sqrt(square_sum / WIDTH + EPS)
    normed = attn_wide * inverse_rms[:, None] * norm_gain[None, :]
    gate_wide = gate_in.astype(jnp.float32)
    mixed_in = gate_wide * normed
    taps = jnp.broadcast_to(
        kernel_taps[:, None, :], (group_count, channels // group_count, FILT)
    ).reshape(channels, FILT)
    rim_before = from_behind(mixed_in[row_count - (FILT - 1) :], "ctx", 1)
    extended = jnp.concatenate([rim_before, mixed_in], axis=0)
    conv_out = jnp.zeros((row_count, channels), jnp.float32)
    for lag in range(FILT):
        conv_out = (
            conv_out + taps[:, lag][None, :] * extended[FILT - 1 - lag : FILT - 1 - lag + row_count]
        )
    out_gate = gate_out.astype(jnp.float32)
    mixed = (out_gate * conv_out).astype(jnp.bfloat16)
    upstream = cotangent.astype(jnp.float32)
    grad_gate_out = (upstream * conv_out).astype(jnp.bfloat16)
    d_conv = upstream * out_gate
    tap_columns = []
    for lag in range(FILT):
        per_channel = jnp.sum(
            d_conv * extended[FILT - 1 - lag : FILT - 1 - lag + row_count], axis=0
        )
        tap_columns.append(per_channel.reshape(group_count, -1).sum(axis=1))
    tap_terms = jnp.stack(tap_columns, axis=1)
    rim_after = from_behind(d_conv[: FILT - 1], "ctx", -1)
    extended_grad = jnp.concatenate([d_conv, rim_after], axis=0)
    d_mixed = jnp.zeros((row_count, channels), jnp.float32)
    for lag in range(FILT):
        d_mixed = d_mixed + taps[:, lag][None, :] * extended_grad[lag : lag + row_count]
    grad_gate_in = (d_mixed * normed).astype(jnp.bfloat16)
    d_normed = d_mixed * gate_wide
    gain_terms = jnp.sum(d_normed * attn_wide * inverse_rms[:, None], axis=0)
    grad_filter, grad_gain = lax.psum((tap_terms, gain_terms), "ctx")
    scaled = d_normed * norm_gain[None, :]
    row_dot = lax.psum(jnp.sum(scaled * attn_wide, axis=1), "chan")
    d_attn = (
        inverse_rms[:, None] * scaled - attn_wide * (inverse_rms**3 * row_dot / WIDTH)[:, None]
    ).astype(jnp.bfloat16)
    d_heads = d_attn.reshape(row_count, head_count, HEAD)
    delta_rows = jnp.sum(
        d_heads.astype(jnp.float32) * attn_wide.reshape(row_count, head_count, HEAD), axis=2
    )
    own_count = (own_first + row_count - 1) // block_rows + 1
    grad_queries = query_grads(
        queries.reshape(row_count, head_count, HEAD),
        d_heads,
        own_first + local_pos,
        own_count,
        keys_heads,
        values_heads,
        lse_rows.T,
        delta_rows.T,
        block_rows,
    )
    lse_all, delta_all = (
        lax.all_gather(lse_rows, "ctx", axis=0, tiled=True),
        lax.all_gather(delta_rows, "ctx", axis=0, tiled=True),
    )
    own_keys = key_rows.reshape(row_count, head_count, HEAD)
    own_values = value_rows.reshape(row_count, head_count, HEAD)
    key_pos = own_first + local_pos
    empty_grad = jnp.zeros((row_count, head_count, HEAD), jnp.float32)
    query_piece = lax.all_gather(queries, "ctx", axis=0, tiled=True)
    d_piece = lax.all_gather(d_attn, "ctx", axis=0, tiled=True)
    piece_rows = query_piece.shape[0]

    def contribute(totals):
        query_heads = query_piece.reshape(piece_rows, head_count, HEAD)
        piece_heads = d_piece.reshape(piece_rows, head_count, HEAD)
        query_pos = jnp.arange(piece_rows, dtype=jnp.int32)
        lse_piece = lse_all.T
        delta_piece = delta_all.T
        scores = score_block(query_heads, own_keys, query_pos, key_pos)
        weights = jnp.exp(scores - lse_piece[:, :, None])
        d_probs = jnp.einsum(
            "rhe,khe->hrk", piece_heads, own_values, preferred_element_type=jnp.float32
        )
        d_scores = (weights * (d_probs - delta_piece[:, :, None])).astype(jnp.bfloat16)
        key_grad = jnp.einsum(
            "hrk,rhe->khe", d_scores, query_heads, preferred_element_type=jnp.float32
        )
        value_grad = jnp.einsum(
            "hrk,rhe->khe",
            weights.astype(jnp.bfloat16),
            piece_heads,
            preferred_element_type=jnp.float32,
        )
        return (key_grad, value_grad)

    def unchanged(totals):
        return totals

    key_grad, value_grad = lax.cond(
        jnp.int32(0) + piece_rows > own_first, contribute, unchanged, (empty_grad, empty_grad)
    )
    grad_keys = (key_grad * HEAD ** (-0.5)).reshape(row_count, channels).astype(jnp.bfloat16)
    grad_values = value_grad.reshape(row_count, channels).astype(jnp.bfloat16)
    return (
        mixed,
        grad_queries,
        grad_keys,
        grad_values,
        grad_gate_in,
        grad_gate_out,
        grad_filter,
        grad_gain,
    )


LOG2E = 1.4426950408889634
VMEM_LIMIT = 20 * 1024 * 1024
PACK_LIMIT = 60 * 1024 * 1024


def vmem_call(body, ins, outs, scratch=(), limit=VMEM_LIMIT, **extra):
    return pl.pallas_call(
        body,
        in_specs=ins,
        out_specs=tuple(spec for spec, _ in outs),
        out_shape=tuple(shape for _, shape in outs),
        scratch_shapes=list(scratch),
        compiler_params=pltpu.CompilerParams(vmem_limit_bytes=limit),
        **extra,
    )


def other(axis, by):
    size = lax.axis_size(axis)
    return lax.rem(lax.axis_index(axis) + by + size, size)


def start_all(copies):
    copies = list(copies)
    for copy in copies:
        copy.start()
    return copies


def wait_all(copies):
    for copy in copies:
        copy.wait()


def arrive(axis, pieces, held):
    for s, piece in enumerate(pieces):
        held[other(axis, -s)] = piece[...]


def depart(axis, held, pieces):
    for s, piece in enumerate(pieces):
        piece[...] = held[other(axis, s)]


def exchange(pieces, axis):
    size = lax.axis_size(axis)
    return [pieces[0]] + [
        lax.ppermute(pieces[s], axis, [(i, (i + s) % size) for i in range(size)])
        for s in range(1, size)
    ]


def dot_nt(a, b, precision=None):
    return lax.dot_general(
        a, b, (((1,), (1,)), ((), ())), precision=precision, preferred_element_type=jnp.float32
    )


def dot_nn(a, b):
    return lax.dot_general(a, b, (((1,), (0,)), ((), ())), preferred_element_type=jnp.float32)


def row_sums_as_lanes(product):
    ones = jnp.ones((8, product.shape[1]), jnp.float32)
    return dot_nt(ones, product, lax.Precision.HIGHEST)[0:1]


def channel_taps(taps_ref, head):
    groups = taps_ref.shape[1]
    size = HEAD * lax.axis_size("ctx") // groups
    wanted = head * (HEAD // size) + lax.broadcasted_iota(jnp.int32, (groups, HEAD), 1) // size
    spread = (wanted == lax.broadcasted_iota(jnp.int32, (groups, HEAD), 0)).astype(jnp.float32)
    return lax.dot_general(
        taps_ref[...],
        spread,
        (((1,), (0,)), ((), ())),
        precision=lax.Precision.HIGHEST,
        preferred_element_type=jnp.float32,
    )


def pack_body(axis, q_ref, k_ref, v_ref, gi_ref, go_ref, ct_ref, taps_ref, gain_ref, *refs):
    blocks = lax.axis_size(axis)
    outs, (coef_ref, go_buf, ct_buf, sems, late) = refs[:blocks], refs[blocks:]
    rows = q_ref.shape[0]
    gates = start_all(
        [
            pltpu.make_async_copy(go_ref, go_buf, late.at[0]),
            pltpu.make_async_copy(ct_ref, ct_buf, late.at[1]),
        ]
    )
    moves = []
    for s, out_ref in enumerate(outs):
        cols = pl.ds(pl.multiple_of(other(axis, s) * HEAD, HEAD), HEAD)
        for at, ref in enumerate((q_ref, k_ref, v_ref, gi_ref)):
            moves.append(
                pltpu.make_async_copy(
                    ref.at[:, cols], out_ref.at[at * rows : (at + 1) * rows, :], sems.at[at, s]
                )
            )
    start_all(moves)
    head = lax.axis_index(axis)
    coef_ref[0:FILT, :] = channel_taps(taps_ref, head)
    coef_ref[FILT : FILT + 1, :] = gain_ref[pl.ds(head, 1), :]
    wait_all(gates)
    for s, out_ref in enumerate(outs):
        cols = pl.ds(pl.multiple_of(other(axis, s) * HEAD, HEAD), HEAD)
        d_conv = go_buf[:, cols].astype(jnp.float32) * ct_buf[:, cols].astype(jnp.float32)
        out_ref[4 * rows : 5 * rows, :] = d_conv.astype(jnp.bfloat16)
    wait_all(moves)


def forward_body(axis, *refs):
    blocks = lax.axis_size(axis)
    pieces, refs = refs[:blocks], refs[blocks:]
    coef_ref, p_ref, attn_ref, dz_ref, pay_ref, du_pad, sums, rx_ref = refs
    arrive(axis, pieces, rx_ref)
    rows = rx_ref.shape[1] // 5
    tokens = blocks * rows
    wide = 2 * rows if blocks % 2 == 0 else rows
    per = wide // rows
    taps = coef_ref[0:FILT, :]
    gain = coef_ref[FILT : FILT + 1, :]

    def part(at, first, count):
        return rx_ref[first : first + count, at * rows : (at + 1) * rows, :].reshape(count * rows, HEAD)

    v_t = part(2, 0, blocks).astype(jnp.float32).T.astype(jnp.bfloat16)
    for b in range(blocks):
        du_pad[b * rows : (b + 1) * rows, :] = part(4, b, 1).astype(jnp.float32)
    du_pad[tokens : tokens + 8, :] = jnp.zeros((8, HEAD), jnp.float32)
    scale = HEAD ** (-0.5) * LOG2E
    for i in range(tokens // wide):
        keys = (i + 1) * wide
        q_i = part(0, i * per, per)
        s = dot_nt(part(1, 0, (i + 1) * per), q_i)
        key_pos = lax.broadcasted_iota(jnp.int32, (wide, wide), 0)
        query_pos = lax.broadcasted_iota(jnp.int32, (wide, wide), 1)
        edge = jnp.where(key_pos <= query_pos, s[keys - wide :], NEG)
        s = edge if i == 0 else jnp.concatenate([s[: keys - wide], edge], axis=0)
        top = jnp.max(s, axis=0, keepdims=True)
        e = jnp.exp2((s - top) * scale)
        p = (e * (1.0 / jnp.sum(e, axis=0, keepdims=True))).astype(jnp.bfloat16)
        p_ref[:keys, i * wide : (i + 1) * wide] = p
        attn_t = dot_nn(v_t[:, :keys], p).astype(jnp.bfloat16).astype(jnp.float32)
        squares = jnp.sum(attn_t * attn_t, axis=0, keepdims=True)
        attn = attn_t.T
        first = i * wide
        attn_ref[first : first + wide, :] = attn.astype(jnp.bfloat16)
        dz = jnp.zeros((wide, HEAD), jnp.float32)
        for lag in range(FILT):
            dz = dz + taps[lag : lag + 1, :] * du_pad[first + lag : first + lag + wide, :]
        dz_ref[first : first + wide, :] = dz
        scaled = dz * part(3, i * per, per).astype(jnp.float32) * gain
        dots = row_sums_as_lanes(scaled * attn)
        for j in range(per):
            at = i * per + j
            sums[at : at + 1, :] = squares[:, j * rows : (j + 1) * rows]
            sums[blocks + at : blocks + at + 1, :] = dots[:, j * rows : (j + 1) * rows]
    low = sums[...].astype(jnp.bfloat16)
    for d in range(pay_ref.shape[0]):
        pay_ref[d] = low


def backward_body(axis, width, *refs):
    blocks = lax.axis_size(axis)
    pieces, refs = refs[:blocks], refs[blocks:]
    rs_ref, coef_ref, p_ref, attn_ref, dz_ref = refs[:5]
    outs, (z_pad, ds_ref, da_ref, dl_ref, rx_ref, out_ref) = refs[5 : 5 + blocks], refs[5 + blocks :]
    arrive(axis, pieces, rx_ref)
    rows = rx_ref.shape[1] // 5
    tokens = blocks * rows
    wide = 2 * rows if blocks % 2 == 0 else rows
    per = wide // rows
    taps = coef_ref[0:FILT, :]
    gain = coef_ref[FILT : FILT + 1, :]

    def part(at, first, count):
        return rx_ref[first : first + count, at * rows : (at + 1) * rows, :].reshape(count * rows, HEAD)

    totals = jnp.sum(rs_ref[...].astype(jnp.float32), axis=0)
    rstd_lanes = 1.0 / jnp.sqrt(totals[:blocks] / width + EPS)
    pull_lanes = rstd_lanes * rstd_lanes * rstd_lanes * totals[blocks:] / width
    z_pad[0:8, :] = jnp.zeros((8, HEAD), jnp.float32)
    grads = [jnp.zeros((1, HEAD), jnp.float32) for _ in range(FILT + 1)]
    for b in range(blocks):
        first = b * rows
        rstd = jnp.broadcast_to(rstd_lanes[b : b + 1], (HEAD, rows)).T
        pull = jnp.broadcast_to(pull_lanes[b : b + 1], (HEAD, rows)).T
        attn = attn_ref[first : first + rows, :].astype(jnp.float32)
        dz = dz_ref[first : first + rows, :]
        gi = part(3, b, 1).astype(jnp.float32)
        du = part(4, b, 1).astype(jnp.float32)
        normed = attn * rstd * gain
        z_pad[8 + first : 8 + first + rows, :] = gi * normed
        conv = jnp.zeros((rows, HEAD), jnp.float32)
        for lag in range(FILT):
            z = z_pad[8 + first - lag : 8 + first - lag + rows, :]
            conv = conv + taps[lag : lag + 1, :] * z
            grads[lag] = grads[lag] + jnp.sum(du * z, axis=0, keepdims=True)
        d_normed = dz * gi
        grads[FILT] = grads[FILT] + jnp.sum(d_normed * attn * rstd, axis=0, keepdims=True)
        d_attn = (rstd * (d_normed * gain) - attn * pull).astype(jnp.bfloat16)
        da_ref[first : first + rows, :] = d_attn
        dl_ref[0:1, first : first + rows] = row_sums_as_lanes(d_attn.astype(jnp.float32) * attn)
        out_ref[b, 3 * rows : 4 * rows, :] = conv.astype(jnp.bfloat16)
        out_ref[b, 4 * rows : 5 * rows, :] = (dz * normed).astype(jnp.bfloat16)
    both = jnp.concatenate(grads, axis=0)
    high = both.astype(jnp.bfloat16).astype(jnp.float32)
    both = jnp.concatenate([high, both - high], axis=0).astype(jnp.bfloat16)
    for b in range(blocks):
        out_ref[b, 5 * rows : 5 * rows + 16, :] = both
    scale = HEAD ** (-0.5)
    k_t = part(1, 0, blocks).astype(jnp.float32).T.astype(jnp.bfloat16)
    for i in range(tokens // wide):
        first, keys = i * wide, (i + 1) * wide
        dp = dot_nt(part(2, 0, (i + 1) * per), da_ref[first : first + wide, :])
        p = p_ref[:keys, first : first + wide].astype(jnp.float32)
        ds = (p * (dp - dl_ref[0:1, first : first + wide])).astype(jnp.bfloat16)
        ds_ref[:keys, first : first + wide] = ds
        gq = (dot_nn(k_t[:, :keys], ds) * scale).T.astype(jnp.bfloat16)
        for j in range(per):
            out_ref[i * per + j, 0:rows, :] = gq[j * rows : (j + 1) * rows]
    for i in range(tokens // wide):
        first = i * wide
        q = part(0, i * per, blocks - i * per)
        gk = (dot_nn(ds_ref[first : first + wide, first:], q) * scale).astype(jnp.bfloat16)
        gv = dot_nn(p_ref[first : first + wide, first:], da_ref[first:, :]).astype(jnp.bfloat16)
        for j in range(per):
            out_ref[i * per + j, rows : 2 * rows, :] = gk[j * rows : (j + 1) * rows]
            out_ref[i * per + j, 2 * rows : 3 * rows, :] = gv[j * rows : (j + 1) * rows]
    depart(axis, out_ref, outs)


def unpack_body(axis, *refs):
    heads = lax.axis_size(axis)
    pieces, refs = refs[:heads], refs[heads:]
    go_ref, ct_ref, mix_ref, gq_ref, gk_ref, gv_ref, ggi_ref, ggo_ref, gf_ref, gg_ref = refs[:10]
    *bufs, sems = refs[10:]
    rows = mix_ref.shape[0]
    outs = (gq_ref, gk_ref, gv_ref, ggi_ref, mix_ref, ggo_ref)
    leaving = [
        pltpu.make_async_copy(buf, ref, sems.at[at]) for at, (buf, ref) in enumerate(zip(bufs, outs))
    ]
    columns = [pl.ds(pl.multiple_of(other(axis, -s) * HEAD, HEAD), HEAD) for s in range(heads)]
    for at, first in enumerate((0, 1, 2, 4)):
        for s, piece in enumerate(pieces):
            bufs[at][:, columns[s]] = piece[first * rows : (first + 1) * rows, :]
        leaving[at].start()
    for at, ref in ((4, go_ref), (5, ct_ref)):
        for s, piece in enumerate(pieces):
            conv = piece[3 * rows : 4 * rows, :].astype(jnp.float32)
            gate = ref[:, columns[s]].astype(jnp.float32)
            bufs[at][:, columns[s]] = (gate * conv).astype(jnp.bfloat16)
        leaving[at].start()
    groups = gf_ref.shape[1]
    size = HEAD * heads // groups
    channel = lax.broadcasted_iota(jnp.int32, (HEAD, groups), 0)
    group = lax.broadcasted_iota(jnp.int32, (HEAD, groups), 1)
    totals = jnp.zeros((16, groups), jnp.float32)
    for s, piece in enumerate(pieces):
        head = other(axis, -s)
        both = piece[5 * rows : 5 * rows + 16, :]
        gather = (head * (HEAD // size) + channel // size == group).astype(jnp.bfloat16)
        totals = totals + dot_nn(both, gather)
        wide = both.astype(jnp.float32)
        gg_ref[pl.ds(head, 1), :] = wide[FILT : FILT + 1] + wide[8 + FILT : 8 + FILT + 1]
    gf_ref[...] = totals[:FILT] + totals[8 : 8 + FILT]
    wait_all(leaving)


def shards_by_heads(
    queries, key_rows, value_rows, gate_in, gate_out, kernel_taps, norm_gain, cotangent
):
    rows, channels = queries.shape
    heads = channels // HEAD
    tokens = rows * heads
    everyone = lax.axis_size("ctx") * lax.axis_size("chan")
    low, full = jnp.bfloat16, jnp.float32
    near, far = pl.BlockSpec(memory_space=pltpu.VMEM), pl.BlockSpec(memory_space=pl.ANY)
    hbm = pl.BlockSpec(memory_space=pltpu.HBM)

    def here(shape, dtype):
        return near, jax.ShapeDtypeStruct(shape, dtype)

    def there(shape, dtype):
        return far, jax.ShapeDtypeStruct(shape, dtype)

    gain = norm_gain.reshape(heads, HEAD)
    taps = kernel_taps.T
    late = pltpu.SemaphoreType.DMA((2,))
    flat = pltpu.VMEM((rows, channels), low)
    *packed, coef = vmem_call(
        functools.partial(pack_body, "ctx"),
        [hbm] * 6 + [near] * 2,
        [here((5 * rows, HEAD), low)] * heads + [here((8, HEAD), full)],
        [flat, flat, pltpu.SemaphoreType.DMA((4, heads)), late],
        limit=PACK_LIMIT,
    )(queries, key_rows, value_rows, gate_in, gate_out, cotangent, taps, gain)
    mine = exchange(packed, "ctx")
    probs, attn, d_mixed, partial = vmem_call(
        functools.partial(forward_body, "ctx"),
        [near] * (heads + 1),
        [
            here((tokens, tokens), low),
            here((tokens, HEAD), low),
            here((tokens, HEAD), full),
            here((everyone, 2 * heads, rows), low),
        ],
        [
            pltpu.VMEM((tokens + 8, HEAD), full),
            pltpu.VMEM((2 * heads, rows), full),
            pltpu.VMEM((heads, 5 * rows, HEAD), low),
        ],
    )(*mine, coef)
    sums = lax.all_to_all(partial, ("ctx", "chan"), 0, 0, tiled=True)
    grads = vmem_call(
        functools.partial(backward_body, "ctx", channels * lax.axis_size("chan")),
        [near] * (heads + 5),
        [here((5 * rows + 16, HEAD), low)] * heads,
        [
            pltpu.VMEM((tokens + 8, HEAD), full),
            pltpu.VMEM((tokens, tokens), low),
            pltpu.VMEM((tokens, HEAD), low),
            pltpu.VMEM((8, tokens), full),
            pltpu.VMEM((heads, 5 * rows, HEAD), low),
            pltpu.VMEM((heads, 5 * rows + 16, HEAD), low),
        ],
    )(*mine, sums, coef, probs, attn, d_mixed)
    back = exchange(grads, "ctx")
    spread = (hbm, jax.ShapeDtypeStruct((rows, channels), low))
    mixed, gq, gk, gv, ggi, ggo, gf, gg = vmem_call(
        functools.partial(unpack_body, "ctx"),
        [near] * (heads + 2),
        [spread] * 6 + [here(kernel_taps.shape[::-1], full), here((heads, HEAD), full)],
        [flat] * 6 + [pltpu.SemaphoreType.DMA((6,))],
    )(*back, gate_out, cotangent)
    return (mixed, gq, gk, gv, ggi, ggo, gf.T, gg.reshape(channels))


def shards(queries, *rest):
    rows, channels = queries.shape
    by_heads = channels // HEAD == lax.axis_size("ctx") and rows == HEAD
    return (shards_by_heads if by_heads else shards_by_rows)(queries, *rest)


def solution(mesh):
    placed = (
        P("ctx", "chan"),
        P("ctx", "chan"),
        P("ctx", "chan"),
        P("ctx", "chan"),
        P("ctx", "chan"),
        P("chan", None),
        P("chan"),
        P("ctx", "chan"),
    )
    return jax.shard_map(
        shards,
        mesh=mesh,
        in_specs=placed,
        out_specs=(
            P("ctx", "chan"),
            P("ctx", "chan"),
            P("ctx", "chan"),
            P("ctx", "chan"),
            P("ctx", "chan"),
            P("ctx", "chan"),
            P("chan", None),
            P("chan"),
        ),
        check_vma=False,
    )
```

```python
import functools

import jax
import jax.numpy as jnp
from jax import lax
from jax.experimental import pallas as pl
from jax.experimental.pallas import tpu as pltpu
from jax.sharding import PartitionSpec as P

HEAD = 128
FILT = 7
WIDTH = 4096


EPS = 1e-06
NEG = -1e30


def from_behind(shard, axis, by):
    length = lax.axis_size(axis)
    pairs = [(i, i + by) for i in range(length) if 0 <= i + by < length]
    return lax.ppermute(shard, axis, pairs)


def score_block(query_heads, key_block, query_pos, key_pos):
    scores = jnp.einsum(
        "rhe,khe->hrk", query_heads, key_block, preferred_element_type=jnp.float32
    ) * HEAD ** (-0.5)
    allowed = query_pos[:, None] >= key_pos[None, :]
    return jnp.where(allowed[None], scores, NEG)


def row_totals(query_heads, query_pos, block_count, keys_heads, block_rows):
    row_count = query_heads.shape[0]
    head_count = query_heads.shape[1]

    def advance(block_index, running):
        row_max, row_sum = running
        first_key = block_index * block_rows
        key_block = lax.dynamic_slice_in_dim(keys_heads, first_key, block_rows, 0)
        key_pos = first_key + jnp.arange(block_rows, dtype=jnp.int32)
        scores = score_block(query_heads, key_block, query_pos, key_pos)
        new_max = jnp.maximum(row_max, jnp.max(scores, axis=2))
        row_sum = row_sum * jnp.exp(row_max - new_max) + jnp.sum(
            jnp.exp(scores - new_max[:, :, None]), axis=2
        )
        return (new_max, row_sum)

    initial = (
        jnp.full((head_count, row_count), NEG, jnp.float32),
        jnp.zeros((head_count, row_count), jnp.float32),
    )
    row_max, row_sum = lax.fori_loop(0, block_count, advance, initial)
    return row_max + jnp.log(row_sum)


def row_outputs(query_heads, query_pos, block_count, keys_heads, values_heads, lse, block_rows):
    row_count = query_heads.shape[0]
    head_count = query_heads.shape[1]

    def advance(block_index, summed):
        first_key = block_index * block_rows
        key_block = lax.dynamic_slice_in_dim(keys_heads, first_key, block_rows, 0)
        value_block = lax.dynamic_slice_in_dim(values_heads, first_key, block_rows, 0)
        key_pos = first_key + jnp.arange(block_rows, dtype=jnp.int32)
        scores = score_block(query_heads, key_block, query_pos, key_pos)
        weights_low = jnp.exp(scores - lse[:, :, None]).astype(jnp.bfloat16)
        return summed + jnp.einsum(
            "hrk,khe->rhe", weights_low, value_block, preferred_element_type=jnp.float32
        )

    summed = lax.fori_loop(
        0, block_count, advance, jnp.zeros((row_count, head_count, HEAD), jnp.float32)
    )
    return summed.reshape(row_count, head_count * HEAD).astype(jnp.bfloat16)


def query_grads(
    query_heads, d_heads, query_pos, block_count, keys_heads, values_heads, lse, delta, block_rows
):
    row_count = query_heads.shape[0]
    head_count = query_heads.shape[1]

    def advance(block_index, summed):
        first_key = block_index * block_rows
        key_block = lax.dynamic_slice_in_dim(keys_heads, first_key, block_rows, 0)
        value_block = lax.dynamic_slice_in_dim(values_heads, first_key, block_rows, 0)
        key_pos = first_key + jnp.arange(block_rows, dtype=jnp.int32)
        scores = score_block(query_heads, key_block, query_pos, key_pos)
        weights = jnp.exp(scores - lse[:, :, None])
        d_probs = jnp.einsum(
            "rhe,khe->hrk", d_heads, value_block, preferred_element_type=jnp.float32
        )
        d_scores = (weights * (d_probs - delta[:, :, None])).astype(jnp.bfloat16)
        return summed + jnp.einsum(
            "hrk,khe->rhe", d_scores, key_block, preferred_element_type=jnp.float32
        )

    summed = lax.fori_loop(
        0, block_count, advance, jnp.zeros((row_count, head_count, HEAD), jnp.float32)
    )
    return (summed * HEAD ** (-0.5)).reshape(row_count, head_count * HEAD).astype(jnp.bfloat16)


def shards_by_rows(queries, key_rows, value_rows, gate_in, gate_out, kernel_taps, norm_gain, cotangent):
    row_count = queries.shape[0]
    channels = queries.shape[1]
    head_count = channels // HEAD
    group_count = kernel_taps.shape[0]
    devices = lax.axis_size("ctx")
    position = lax.axis_index("ctx")
    own_first = position * row_count
    total_rows = row_count * devices
    block_rows = min(512, total_rows)
    local_pos = jnp.arange(row_count, dtype=jnp.int32)
    keys_all, values_all = (
        lax.all_gather(key_rows, "ctx", axis=0, tiled=True),
        lax.all_gather(value_rows, "ctx", axis=0, tiled=True),
    )
    keys_heads = keys_all.reshape(total_rows, head_count, HEAD)
    query_sets = (queries, own_first + local_pos)
    query_block, query_pos = query_sets
    block_count = query_pos[-1] // block_rows + 1
    lse_sets = row_totals(
        query_block.reshape(-1, head_count, HEAD), query_pos, block_count, keys_heads, block_rows
    )
    values_heads = values_all.reshape(total_rows, head_count, HEAD)
    query_block, query_pos = query_sets
    outputs = row_outputs(
        query_block.reshape(-1, head_count, HEAD),
        query_pos,
        block_count,
        keys_heads,
        values_heads,
        lse_sets,
        block_rows,
    )
    lse_rows = lse_sets.T
    attn_wide = outputs.astype(jnp.float32)
    square_sum = lax.psum(jnp.sum(attn_wide * attn_wide, axis=1), "chan")
    inverse_rms = 1.0 / jnp.sqrt(square_sum / WIDTH + EPS)
    normed = attn_wide * inverse_rms[:, None] * norm_gain[None, :]
    gate_wide = gate_in.astype(jnp.float32)
    mixed_in = gate_wide * normed
    taps = jnp.broadcast_to(
        kernel_taps[:, None, :], (group_count, channels // group_count, FILT)
    ).reshape(channels, FILT)
    rim_before = from_behind(mixed_in[row_count - (FILT - 1) :], "ctx", 1)
    extended = jnp.concatenate([rim_before, mixed_in], axis=0)
    conv_out = jnp.zeros((row_count, channels), jnp.float32)
    for lag in range(FILT):
        conv_out = (
            conv_out + taps[:, lag][None, :] * extended[FILT - 1 - lag : FILT - 1 - lag + row_count]
        )
    out_gate = gate_out.astype(jnp.float32)
    mixed = (out_gate * conv_out).astype(jnp.bfloat16)
    upstream = cotangent.astype(jnp.float32)
    grad_gate_out = (upstream * conv_out).astype(jnp.bfloat16)
    d_conv = upstream * out_gate
    tap_columns = []
    for lag in range(FILT):
        per_channel = jnp.sum(
            d_conv * extended[FILT - 1 - lag : FILT - 1 - lag + row_count], axis=0
        )
        tap_columns.append(per_channel.reshape(group_count, -1).sum(axis=1))
    tap_terms = jnp.stack(tap_columns, axis=1)
    rim_after = from_behind(d_conv[: FILT - 1], "ctx", -1)
    extended_grad = jnp.concatenate([d_conv, rim_after], axis=0)
    d_mixed = jnp.zeros((row_count, channels), jnp.float32)
    for lag in range(FILT):
        d_mixed = d_mixed + taps[:, lag][None, :] * extended_grad[lag : lag + row_count]
    grad_gate_in = (d_mixed * normed).astype(jnp.bfloat16)
    d_normed = d_mixed * gate_wide
    gain_terms = jnp.sum(d_normed * attn_wide * inverse_rms[:, None], axis=0)
    grad_filter, grad_gain = lax.psum((tap_terms, gain_terms), "ctx")
    scaled = d_normed * norm_gain[None, :]
    row_dot = lax.psum(jnp.sum(scaled * attn_wide, axis=1), "chan")
    d_attn = (
        inverse_rms[:, None] * scaled - attn_wide * (inverse_rms**3 * row_dot / WIDTH)[:, None]
    ).astype(jnp.bfloat16)
    d_heads = d_attn.reshape(row_count, head_count, HEAD)
    delta_rows = jnp.sum(
        d_heads.astype(jnp.float32) * attn_wide.reshape(row_count, head_count, HEAD), axis=2
    )
    own_count = (own_first + row_count - 1) // block_rows + 1
    grad_queries = query_grads(
        queries.reshape(row_count, head_count, HEAD),
        d_heads,
        own_first + local_pos,
        own_count,
        keys_heads,
        values_heads,
        lse_rows.T,
        delta_rows.T,
        block_rows,
    )
    lse_all, delta_all = (
        lax.all_gather(lse_rows, "ctx", axis=0, tiled=True),
        lax.all_gather(delta_rows, "ctx", axis=0, tiled=True),
    )
    own_keys = key_rows.reshape(row_count, head_count, HEAD)
    own_values = value_rows.reshape(row_count, head_count, HEAD)
    key_pos = own_first + local_pos
    empty_grad = jnp.zeros((row_count, head_count, HEAD), jnp.float32)
    query_piece = lax.all_gather(queries, "ctx", axis=0, tiled=True)
    d_piece = lax.all_gather(d_attn, "ctx", axis=0, tiled=True)
    piece_rows = query_piece.shape[0]

    def contribute(totals):
        query_heads = query_piece.reshape(piece_rows, head_count, HEAD)
        piece_heads = d_piece.reshape(piece_rows, head_count, HEAD)
        query_pos = jnp.arange(piece_rows, dtype=jnp.int32)
        lse_piece = lse_all.T
        delta_piece = delta_all.T
        scores = score_block(query_heads, own_keys, query_pos, key_pos)
        weights = jnp.exp(scores - lse_piece[:, :, None])
        d_probs = jnp.einsum(
            "rhe,khe->hrk", piece_heads, own_values, preferred_element_type=jnp.float32
        )
        d_scores = (weights * (d_probs - delta_piece[:, :, None])).astype(jnp.bfloat16)
        key_grad = jnp.einsum(
            "hrk,rhe->khe", d_scores, query_heads, preferred_element_type=jnp.float32
        )
        value_grad = jnp.einsum(
            "hrk,rhe->khe",
            weights.astype(jnp.bfloat16),
            piece_heads,
            preferred_element_type=jnp.float32,
        )
        return (key_grad, value_grad)

    def unchanged(totals):
        return totals

    key_grad, value_grad = lax.cond(
        jnp.int32(0) + piece_rows > own_first, contribute, unchanged, (empty_grad, empty_grad)
    )
    grad_keys = (key_grad * HEAD ** (-0.5)).reshape(row_count, channels).astype(jnp.bfloat16)
    grad_values = value_grad.reshape(row_count, channels).astype(jnp.bfloat16)
    return (
        mixed,
        grad_queries,
        grad_keys,
        grad_values,
        grad_gate_in,
        grad_gate_out,
        grad_filter,
        grad_gain,
    )


LOG2E = 1.4426950408889634
VMEM_LIMIT = 20 * 1024 * 1024
PACK_LIMIT = 54600 * 1024


def vmem_call(body, ins, outs, scratch=(), limit=VMEM_LIMIT, **extra):
    return pl.pallas_call(
        body,
        in_specs=ins,
        out_specs=tuple(spec for spec, _ in outs),
        out_shape=tuple(shape for _, shape in outs),
        scratch_shapes=list(scratch),
        compiler_params=pltpu.CompilerParams(vmem_limit_bytes=limit),
        **extra,
    )


def other(axis, by):
    size = lax.axis_size(axis)
    return lax.rem(lax.axis_index(axis) + by + size, size)


def start_all(copies):
    copies = list(copies)
    for copy in copies:
        copy.start()
    return copies


def wait_all(copies):
    for copy in copies:
        copy.wait()


def arrive(axis, pieces, held):
    for s, piece in enumerate(pieces):
        held[other(axis, -s)] = piece[...]


def depart(axis, held, pieces):
    for s, piece in enumerate(pieces):
        piece[...] = held[other(axis, s)]


def exchange(pieces, axis):
    size = lax.axis_size(axis)
    return [pieces[0]] + [
        lax.ppermute(pieces[s], axis, [(i, (i + s) % size) for i in range(size)])
        for s in range(1, size)
    ]


def dot_nt(a, b, precision=None):
    return lax.dot_general(
        a, b, (((1,), (1,)), ((), ())), precision=precision, preferred_element_type=jnp.float32
    )


def dot_nn(a, b):
    return lax.dot_general(a, b, (((1,), (0,)), ((), ())), preferred_element_type=jnp.float32)


def row_sums_as_lanes(product):
    ones = jnp.ones((8, product.shape[1]), jnp.float32)
    return dot_nt(ones, product, lax.Precision.HIGHEST)[0:1]


def channel_taps(taps_ref, head):
    groups = taps_ref.shape[1]
    size = HEAD * lax.axis_size("ctx") // groups
    wanted = head * (HEAD // size) + lax.broadcasted_iota(jnp.int32, (groups, HEAD), 1) // size
    spread = (wanted == lax.broadcasted_iota(jnp.int32, (groups, HEAD), 0)).astype(jnp.float32)
    return lax.dot_general(
        taps_ref[...],
        spread,
        (((1,), (0,)), ((), ())),
        precision=lax.Precision.HIGHEST,
        preferred_element_type=jnp.float32,
    )


def pack_body(axis, *refs):
    blocks = lax.axis_size(axis)
    arrays, outs, bufs, sems = refs[:6], refs[6 : 6 + blocks], refs[6 + blocks : 12 + blocks], refs[-1]
    rows = arrays[0].shape[0]
    coming = start_all(
        pltpu.make_async_copy(ref, buf, sems.at[at]) for at, (ref, buf) in enumerate(zip(arrays, bufs))
    )
    columns = [pl.ds(pl.multiple_of(other(axis, s) * HEAD, HEAD), HEAD) for s in range(blocks)]
    for at in range(4):
        coming[at].wait()
        for s, out_ref in enumerate(outs):
            out_ref[at * rows : (at + 1) * rows, :] = bufs[at][:, columns[s]]
    wait_all(coming[4:])
    for s, out_ref in enumerate(outs):
        d_conv = bufs[4][:, columns[s]].astype(jnp.float32) * bufs[5][:, columns[s]].astype(jnp.float32)
        out_ref[4 * rows : 5 * rows, :] = d_conv.astype(jnp.bfloat16)


def prepare_body(axis, token_ref, taps_ref, gain_ref, go_ref, ct_ref, coef_ref, wide_ref, dz_ref, du_pad):
    heads = lax.axis_size(axis)
    rows = go_ref.shape[0]
    mine = lax.axis_index(axis)
    coef_ref[0:FILT, :] = channel_taps(taps_ref, mine)
    coef_ref[FILT : FILT + 1, :] = gain_ref[pl.ds(mine, 1), :]
    du_pad[rows : rows + 8, :] = jnp.zeros((8, du_pad.shape[1]), jnp.float32)
    du_pad[0:rows, :] = go_ref[...].astype(jnp.float32) * ct_ref[...].astype(jnp.float32)
    for head in range(heads):
        cols = slice(head * HEAD, (head + 1) * HEAD)
        taps = channel_taps(taps_ref, head)
        wide_ref[0:FILT, cols] = taps
        wide_ref[FILT : FILT + 1, cols] = gain_ref[head : head + 1, :]
        dz = jnp.zeros((rows, HEAD), jnp.float32)
        for lag in range(FILT):
            dz = dz + taps[lag : lag + 1, :] * du_pad[lag : lag + rows, cols]
        dz_ref[:, cols] = dz


def forward_body(axis, *refs):
    blocks = lax.axis_size(axis)
    pieces, refs = refs[:blocks], refs[blocks:]
    coef_ref, p_ref, attn_ref, dz_ref, pay_ref, du_pad, sums, rx_ref = refs
    arrive(axis, pieces, rx_ref)
    rows = rx_ref.shape[1] // 5
    tokens = blocks * rows
    wide = 2 * rows if blocks % 2 == 0 else rows
    per = wide // rows
    taps = coef_ref[0:FILT, :]
    gain = coef_ref[FILT : FILT + 1, :]

    def part(at, first, count):
        return rx_ref[first : first + count, at * rows : (at + 1) * rows, :].reshape(count * rows, HEAD)

    v_t = part(2, 0, blocks).astype(jnp.float32).T.astype(jnp.bfloat16)
    for b in range(blocks):
        du_pad[b * rows : (b + 1) * rows, :] = part(4, b, 1).astype(jnp.float32)
    du_pad[tokens : tokens + 8, :] = jnp.zeros((8, HEAD), jnp.float32)
    scale = HEAD ** (-0.5) * LOG2E
    for i in range(tokens // wide):
        keys = (i + 1) * wide
        q_i = part(0, i * per, per)
        s = dot_nt(part(1, 0, (i + 1) * per), q_i)
        key_pos = lax.broadcasted_iota(jnp.int32, (wide, wide), 0)
        query_pos = lax.broadcasted_iota(jnp.int32, (wide, wide), 1)
        edge = jnp.where(key_pos <= query_pos, s[keys - wide :], NEG)
        s = edge if i == 0 else jnp.concatenate([s[: keys - wide], edge], axis=0)
        top = jnp.max(s, axis=0, keepdims=True)
        e = jnp.exp2((s - top) * scale)
        p = (e * (1.0 / jnp.sum(e, axis=0, keepdims=True))).astype(jnp.bfloat16)
        p_ref[:keys, i * wide : (i + 1) * wide] = p
        attn_t = dot_nn(v_t[:, :keys], p).astype(jnp.bfloat16).astype(jnp.float32)
        squares = jnp.sum(attn_t * attn_t, axis=0, keepdims=True)
        attn = attn_t.T
        first = i * wide
        attn_ref[first : first + wide, :] = attn.astype(jnp.bfloat16)
        dz = jnp.zeros((wide, HEAD), jnp.float32)
        for lag in range(FILT):
            dz = dz + taps[lag : lag + 1, :] * du_pad[first + lag : first + lag + wide, :]
        dz_ref[first : first + wide, :] = dz
        gated = part(3, i * per, per).astype(jnp.float32) * gain
        dots = row_sums_as_lanes(dz * gated * attn)
        for j in range(per):
            at = i * per + j
            sums[at : at + 1, :] = squares[:, j * rows : (j + 1) * rows]
            sums[blocks + at : blocks + at + 1, :] = dots[:, j * rows : (j + 1) * rows]
    low = sums[...].astype(jnp.bfloat16)
    for d in range(pay_ref.shape[0]):
        pay_ref[d] = low


def backward_body(axis, width, *refs):
    blocks = lax.axis_size(axis)
    pieces, refs = refs[:blocks], refs[blocks:]
    rs_ref, coef_ref, p_ref, attn_ref, dz_ref = refs[:5]
    outs, (z_pad, ds_ref, da_ref, dl_ref, rx_ref, out_ref) = refs[5 : 5 + blocks], refs[5 + blocks :]
    arrive(axis, pieces, rx_ref)
    rows = rx_ref.shape[1] // 5
    tokens = blocks * rows
    wide = 2 * rows if blocks % 2 == 0 else rows
    per = wide // rows
    gain = coef_ref[FILT : FILT + 1, :]

    def part(at, first, count):
        return rx_ref[first : first + count, at * rows : (at + 1) * rows, :].reshape(count * rows, HEAD)

    totals = jnp.sum(rs_ref[...].astype(jnp.float32), axis=0)
    rstd_lanes = 1.0 / jnp.sqrt(totals[:blocks] / width + EPS)
    pull_lanes = rstd_lanes * rstd_lanes * rstd_lanes * totals[blocks:] / width
    z_pad[0:8, :] = jnp.zeros((8, HEAD), jnp.float32)
    grads = [jnp.zeros((1, HEAD), jnp.float32) for _ in range(FILT + 1)]
    for b in range(blocks):
        first = b * rows
        rstd = jnp.broadcast_to(rstd_lanes[b : b + 1], (HEAD, rows)).T
        pull = jnp.broadcast_to(pull_lanes[b : b + 1], (HEAD, rows)).T
        attn = attn_ref[first : first + rows, :].astype(jnp.float32)
        dz = dz_ref[first : first + rows, :]
        gi = part(3, b, 1).astype(jnp.float32)
        du = part(4, b, 1).astype(jnp.float32)
        normed = attn * rstd * gain
        z_pad[8 + first : 8 + first + rows, :] = gi * normed
        for lag in range(FILT):
            z = z_pad[8 + first - lag : 8 + first - lag + rows, :]
            grads[lag] = grads[lag] + jnp.sum(du * z, axis=0, keepdims=True)
        out_ref[b, 3 * rows : 4 * rows, :] = normed.astype(jnp.bfloat16)
        edge = jnp.concatenate([z_pad[first : first + 8, :], dz[rows - 8 :]], axis=0)
        out_ref[b, 4 * rows : 4 * rows + 16, :] = edge.astype(jnp.bfloat16)
        d_normed = dz * gi
        grads[FILT] = grads[FILT] + jnp.sum(d_normed * attn * rstd, axis=0, keepdims=True)
        d_attn = (rstd * (d_normed * gain) - attn * pull).astype(jnp.bfloat16)
        da_ref[first : first + rows, :] = d_attn
        dl_ref[0:1, first : first + rows] = row_sums_as_lanes(d_attn.astype(jnp.float32) * attn)
    both = jnp.concatenate(grads, axis=0)
    high = both.astype(jnp.bfloat16).astype(jnp.float32)
    both = jnp.concatenate([high, both - high], axis=0).astype(jnp.bfloat16)
    for b in range(blocks):
        out_ref[b, 4 * rows + 16 : 4 * rows + 32, :] = both
    scale = HEAD ** (-0.5)
    k_t = part(1, 0, blocks).astype(jnp.float32).T.astype(jnp.bfloat16)
    for i in range(tokens // wide):
        first, keys = i * wide, (i + 1) * wide
        dp = dot_nt(part(2, 0, (i + 1) * per), da_ref[first : first + wide, :])
        p = p_ref[:keys, first : first + wide].astype(jnp.float32)
        ds = (p * (dp - dl_ref[0:1, first : first + wide])).astype(jnp.bfloat16)
        ds_ref[:keys, first : first + wide] = ds
        gq = (dot_nn(k_t[:, :keys], ds) * scale).T.astype(jnp.bfloat16)
        for j in range(per):
            out_ref[i * per + j, 0:rows, :] = gq[j * rows : (j + 1) * rows]
    for i in range(tokens // wide):
        first = i * wide
        q = part(0, i * per, blocks - i * per)
        gk = (dot_nn(ds_ref[first : first + wide, first:], q) * scale).astype(jnp.bfloat16)
        gv = dot_nn(p_ref[first : first + wide, first:], da_ref[first:, :]).astype(jnp.bfloat16)
        for j in range(per):
            out_ref[i * per + j, rows : 2 * rows, :] = gk[j * rows : (j + 1) * rows]
            out_ref[i * per + j, 2 * rows : 3 * rows, :] = gv[j * rows : (j + 1) * rows]
    depart(axis, out_ref, outs)


def unpack_body(axis, *refs):
    heads = lax.axis_size(axis)
    pieces, refs = refs[:heads], refs[heads:]
    gi_ref, go_ref, ct_ref, dz_ref, wide_ref = refs[:5]
    outs, (gf_ref, gg_ref), bufs, (z_pad, sems) = refs[5:11], refs[11:13], refs[13:19], refs[19:]
    rows = gi_ref.shape[0]
    leaving = [
        pltpu.make_async_copy(buf, ref, sems.at[at]) for at, (buf, ref) in enumerate(zip(bufs, outs))
    ]
    columns = [pl.ds(pl.multiple_of(other(axis, -s) * HEAD, HEAD), HEAD) for s in range(heads)]
    for at in range(3):
        for s, piece in enumerate(pieces):
            bufs[at][:, columns[s]] = piece[at * rows : (at + 1) * rows, :]
        leaving[at].start()
    for s, piece in enumerate(pieces):
        cols = columns[s]
        edge = piece[4 * rows : 4 * rows + 16, :].astype(jnp.float32)
        normed = piece[3 * rows : 4 * rows, :].astype(jnp.float32)
        z_pad[s, 0:8, :] = edge[0:8]
        z_pad[s, 8 : 8 + rows, :] = gi_ref[:, cols].astype(jnp.float32) * normed
        dz = jnp.concatenate([dz_ref[0 : rows - 8, cols], edge[8:16]], axis=0)
        bufs[3][:, cols] = (dz * normed).astype(jnp.bfloat16)
    leaving[3].start()
    for s in range(heads):
        cols = columns[s]
        conv = jnp.zeros((rows, HEAD), jnp.float32)
        for lag in range(FILT):
            conv = conv + wide_ref[lag : lag + 1, cols] * z_pad[s, 8 - lag : 8 - lag + rows, :]
        bufs[4][:, cols] = (go_ref[:, cols].astype(jnp.float32) * conv).astype(jnp.bfloat16)
        bufs[5][:, cols] = (ct_ref[:, cols].astype(jnp.float32) * conv).astype(jnp.bfloat16)
    leaving[4].start()
    leaving[5].start()
    groups = gf_ref.shape[1]
    size = HEAD * heads // groups
    channel = lax.broadcasted_iota(jnp.int32, (HEAD, groups), 0)
    group = lax.broadcasted_iota(jnp.int32, (HEAD, groups), 1)
    totals = jnp.zeros((16, groups), jnp.float32)
    for s, piece in enumerate(pieces):
        head = other(axis, -s)
        both = piece[4 * rows + 16 : 4 * rows + 32, :]
        gather = (head * (HEAD // size) + channel // size == group).astype(jnp.bfloat16)
        totals = totals + dot_nn(both, gather)
        total = both.astype(jnp.float32)
        gg_ref[pl.ds(head, 1), :] = total[FILT : FILT + 1] + total[8 + FILT : 8 + FILT + 1]
    gf_ref[...] = totals[:FILT] + totals[8 : 8 + FILT]
    wait_all(leaving)


def cost(flops, moved):
    return pl.CostEstimate(flops=flops, bytes_accessed=moved, transcendentals=0)


def shards_by_heads(
    queries, key_rows, value_rows, gate_in, gate_out, kernel_taps, norm_gain, cotangent
):
    rows, channels = queries.shape
    heads = channels // HEAD
    tokens = rows * heads
    everyone = lax.axis_size("ctx") * lax.axis_size("chan")
    low, full = jnp.bfloat16, jnp.float32
    near, far = pl.BlockSpec(memory_space=pltpu.VMEM), pl.BlockSpec(memory_space=pl.ANY)
    hbm = pl.BlockSpec(memory_space=pltpu.HBM)

    def here(shape, dtype):
        return near, jax.ShapeDtypeStruct(shape, dtype)

    def there(shape, dtype):
        return far, jax.ShapeDtypeStruct(shape, dtype)

    gain = norm_gain.reshape(heads, HEAD)
    taps = kernel_taps.T
    flat = pltpu.VMEM((rows, channels), low)
    width = channels * lax.axis_size("chan")
    packed = vmem_call(
        functools.partial(pack_body, "ctx"),
        [hbm] * 6,
        [here((5 * rows, HEAD), low)] * heads,
        [flat] * 6 + [pltpu.SemaphoreType.DMA((6,))],
        limit=PACK_LIMIT,
    )(queries, key_rows, value_rows, gate_in, gate_out, cotangent)
    mine = exchange(packed, "ctx")
    coef, wide, own_d_mixed = vmem_call(
        functools.partial(prepare_body, "ctx"),
        [far] + [near] * 4,
        [here((8, HEAD), full), here((8, channels), full), here((rows, channels), full)],
        [pltpu.VMEM((rows + 8, channels), full)],
        cost_estimate=cost(rows * channels * 20, rows * channels * 32),
    )(packed[0], taps, gain, gate_out, cotangent)
    probs, attn, d_mixed, partial = vmem_call(
        functools.partial(forward_body, "ctx"),
        [near] * (heads + 1),
        [
            here((tokens, tokens), low),
            here((tokens, HEAD), low),
            here((tokens, HEAD), full),
            here((everyone, 2 * heads, rows), low),
        ],
        [
            pltpu.VMEM((tokens + 8, HEAD), full),
            pltpu.VMEM((2 * heads, rows), full),
            pltpu.VMEM((heads, 5 * rows, HEAD), low),
        ],
    )(*mine, coef)
    sums = lax.all_to_all(partial, ("ctx", "chan"), 0, 0, tiled=True)
    grads = vmem_call(
        functools.partial(backward_body, "ctx", width),
        [near] * (heads + 5),
        [here((4 * rows + 32, HEAD), low)] * heads,
        [
            pltpu.VMEM((tokens + 8, HEAD), full),
            pltpu.VMEM((tokens, tokens), low),
            pltpu.VMEM((tokens, HEAD), low),
            pltpu.VMEM((8, tokens), full),
            pltpu.VMEM((heads, 5 * rows, HEAD), low),
            pltpu.VMEM((heads, 4 * rows + 32, HEAD), low),
        ],
    )(*mine, sums, coef, probs, attn, d_mixed)
    back = exchange(grads, "ctx")
    spread = (hbm, jax.ShapeDtypeStruct((rows, channels), low))
    gq, gk, gv, ggi, mixed, ggo, gf, gg = vmem_call(
        functools.partial(unpack_body, "ctx"),
        [near] * (heads + 5),
        [spread] * 6 + [here(kernel_taps.shape[::-1], full), here((heads, HEAD), full)],
        [flat] * 6 + [pltpu.VMEM((heads, rows + 8, HEAD), full), pltpu.SemaphoreType.DMA((6,))],
    )(*back, gate_in, gate_out, cotangent, own_d_mixed, wide)
    return (mixed, gq, gk, gv, ggi, ggo, gf.T, gg.reshape(channels))


def shards(queries, *rest):
    rows, channels = queries.shape
    by_heads = channels // HEAD == lax.axis_size("ctx") and rows == HEAD
    return (shards_by_heads if by_heads else shards_by_rows)(queries, *rest)


def solution(mesh):
    placed = (
        P("ctx", "chan"),
        P("ctx", "chan"),
        P("ctx", "chan"),
        P("ctx", "chan"),
        P("ctx", "chan"),
        P("chan", None),
        P("chan"),
        P("ctx", "chan"),
    )
    return jax.shard_map(
        shards,
        mesh=mesh,
        in_specs=placed,
        out_specs=(
            P("ctx", "chan"),
            P("ctx", "chan"),
            P("ctx", "chan"),
            P("ctx", "chan"),
            P("ctx", "chan"),
            P("ctx", "chan"),
            P("chan", None),
            P("chan"),
        ),
        check_vma=False,
    )
```

```python
import functools

import jax
import jax.numpy as jnp
from jax import lax
from jax.experimental import pallas as pl
from jax.experimental.pallas import tpu as pltpu
from jax.sharding import PartitionSpec as P

HEAD = 128
FILT = 7
WIDTH = 4096


EPS = 1e-06
NEG = -1e30


def from_behind(shard, axis, by):
    length = lax.axis_size(axis)
    pairs = [(i, i + by) for i in range(length) if 0 <= i + by < length]
    return lax.ppermute(shard, axis, pairs)


def score_block(query_heads, key_block, query_pos, key_pos):
    scores = jnp.einsum(
        "rhe,khe->hrk", query_heads, key_block, preferred_element_type=jnp.float32
    ) * HEAD ** (-0.5)
    allowed = query_pos[:, None] >= key_pos[None, :]
    return jnp.where(allowed[None], scores, NEG)


def row_totals(query_heads, query_pos, block_count, keys_heads, block_rows):
    row_count = query_heads.shape[0]
    head_count = query_heads.shape[1]

    def advance(block_index, running):
        row_max, row_sum = running
        first_key = block_index * block_rows
        key_block = lax.dynamic_slice_in_dim(keys_heads, first_key, block_rows, 0)
        key_pos = first_key + jnp.arange(block_rows, dtype=jnp.int32)
        scores = score_block(query_heads, key_block, query_pos, key_pos)
        new_max = jnp.maximum(row_max, jnp.max(scores, axis=2))
        row_sum = row_sum * jnp.exp(row_max - new_max) + jnp.sum(
            jnp.exp(scores - new_max[:, :, None]), axis=2
        )
        return (new_max, row_sum)

    initial = (
        jnp.full((head_count, row_count), NEG, jnp.float32),
        jnp.zeros((head_count, row_count), jnp.float32),
    )
    row_max, row_sum = lax.fori_loop(0, block_count, advance, initial)
    return row_max + jnp.log(row_sum)


def row_outputs(query_heads, query_pos, block_count, keys_heads, values_heads, lse, block_rows):
    row_count = query_heads.shape[0]
    head_count = query_heads.shape[1]

    def advance(block_index, summed):
        first_key = block_index * block_rows
        key_block = lax.dynamic_slice_in_dim(keys_heads, first_key, block_rows, 0)
        value_block = lax.dynamic_slice_in_dim(values_heads, first_key, block_rows, 0)
        key_pos = first_key + jnp.arange(block_rows, dtype=jnp.int32)
        scores = score_block(query_heads, key_block, query_pos, key_pos)
        weights_low = jnp.exp(scores - lse[:, :, None]).astype(jnp.bfloat16)
        return summed + jnp.einsum(
            "hrk,khe->rhe", weights_low, value_block, preferred_element_type=jnp.float32
        )

    summed = lax.fori_loop(
        0, block_count, advance, jnp.zeros((row_count, head_count, HEAD), jnp.float32)
    )
    return summed.reshape(row_count, head_count * HEAD).astype(jnp.bfloat16)


def query_grads(
    query_heads, d_heads, query_pos, block_count, keys_heads, values_heads, lse, delta, block_rows
):
    row_count = query_heads.shape[0]
    head_count = query_heads.shape[1]

    def advance(block_index, summed):
        first_key = block_index * block_rows
        key_block = lax.dynamic_slice_in_dim(keys_heads, first_key, block_rows, 0)
        value_block = lax.dynamic_slice_in_dim(values_heads, first_key, block_rows, 0)
        key_pos = first_key + jnp.arange(block_rows, dtype=jnp.int32)
        scores = score_block(query_heads, key_block, query_pos, key_pos)
        weights = jnp.exp(scores - lse[:, :, None])
        d_probs = jnp.einsum(
            "rhe,khe->hrk", d_heads, value_block, preferred_element_type=jnp.float32
        )
        d_scores = (weights * (d_probs - delta[:, :, None])).astype(jnp.bfloat16)
        return summed + jnp.einsum(
            "hrk,khe->rhe", d_scores, key_block, preferred_element_type=jnp.float32
        )

    summed = lax.fori_loop(
        0, block_count, advance, jnp.zeros((row_count, head_count, HEAD), jnp.float32)
    )
    return (summed * HEAD ** (-0.5)).reshape(row_count, head_count * HEAD).astype(jnp.bfloat16)


def shards_by_rows(queries, key_rows, value_rows, gate_in, gate_out, kernel_taps, norm_gain, cotangent):
    row_count = queries.shape[0]
    channels = queries.shape[1]
    head_count = channels // HEAD
    group_count = kernel_taps.shape[0]
    devices = lax.axis_size("ctx")
    position = lax.axis_index("ctx")
    own_first = position * row_count
    total_rows = row_count * devices
    block_rows = min(512, total_rows)
    local_pos = jnp.arange(row_count, dtype=jnp.int32)
    keys_all, values_all = (
        lax.all_gather(key_rows, "ctx", axis=0, tiled=True),
        lax.all_gather(value_rows, "ctx", axis=0, tiled=True),
    )
    keys_heads = keys_all.reshape(total_rows, head_count, HEAD)
    query_sets = (queries, own_first + local_pos)
    query_block, query_pos = query_sets
    block_count = query_pos[-1] // block_rows + 1
    lse_sets = row_totals(
        query_block.reshape(-1, head_count, HEAD), query_pos, block_count, keys_heads, block_rows
    )
    values_heads = values_all.reshape(total_rows, head_count, HEAD)
    query_block, query_pos = query_sets
    outputs = row_outputs(
        query_block.reshape(-1, head_count, HEAD),
        query_pos,
        block_count,
        keys_heads,
        values_heads,
        lse_sets,
        block_rows,
    )
    lse_rows = lse_sets.T
    attn_wide = outputs.astype(jnp.float32)
    square_sum = lax.psum(jnp.sum(attn_wide * attn_wide, axis=1), "chan")
    inverse_rms = 1.0 / jnp.sqrt(square_sum / WIDTH + EPS)
    normed = attn_wide * inverse_rms[:, None] * norm_gain[None, :]
    gate_wide = gate_in.astype(jnp.float32)
    mixed_in = gate_wide * normed
    taps = jnp.broadcast_to(
        kernel_taps[:, None, :], (group_count, channels // group_count, FILT)
    ).reshape(channels, FILT)
    rim_before = from_behind(mixed_in[row_count - (FILT - 1) :], "ctx", 1)
    extended = jnp.concatenate([rim_before, mixed_in], axis=0)
    conv_out = jnp.zeros((row_count, channels), jnp.float32)
    for lag in range(FILT):
        conv_out = (
            conv_out + taps[:, lag][None, :] * extended[FILT - 1 - lag : FILT - 1 - lag + row_count]
        )
    out_gate = gate_out.astype(jnp.float32)
    mixed = (out_gate * conv_out).astype(jnp.bfloat16)
    upstream = cotangent.astype(jnp.float32)
    grad_gate_out = (upstream * conv_out).astype(jnp.bfloat16)
    d_conv = upstream * out_gate
    tap_columns = []
    for lag in range(FILT):
        per_channel = jnp.sum(
            d_conv * extended[FILT - 1 - lag : FILT - 1 - lag + row_count], axis=0
        )
        tap_columns.append(per_channel.reshape(group_count, -1).sum(axis=1))
    tap_terms = jnp.stack(tap_columns, axis=1)
    rim_after = from_behind(d_conv[: FILT - 1], "ctx", -1)
    extended_grad = jnp.concatenate([d_conv, rim_after], axis=0)
    d_mixed = jnp.zeros((row_count, channels), jnp.float32)
    for lag in range(FILT):
        d_mixed = d_mixed + taps[:, lag][None, :] * extended_grad[lag : lag + row_count]
    grad_gate_in = (d_mixed * normed).astype(jnp.bfloat16)
    d_normed = d_mixed * gate_wide
    gain_terms = jnp.sum(d_normed * attn_wide * inverse_rms[:, None], axis=0)
    grad_filter, grad_gain = lax.psum((tap_terms, gain_terms), "ctx")
    scaled = d_normed * norm_gain[None, :]
    row_dot = lax.psum(jnp.sum(scaled * attn_wide, axis=1), "chan")
    d_attn = (
        inverse_rms[:, None] * scaled - attn_wide * (inverse_rms**3 * row_dot / WIDTH)[:, None]
    ).astype(jnp.bfloat16)
    d_heads = d_attn.reshape(row_count, head_count, HEAD)
    delta_rows = jnp.sum(
        d_heads.astype(jnp.float32) * attn_wide.reshape(row_count, head_count, HEAD), axis=2
    )
    own_count = (own_first + row_count - 1) // block_rows + 1
    grad_queries = query_grads(
        queries.reshape(row_count, head_count, HEAD),
        d_heads,
        own_first + local_pos,
        own_count,
        keys_heads,
        values_heads,
        lse_rows.T,
        delta_rows.T,
        block_rows,
    )
    lse_all, delta_all = (
        lax.all_gather(lse_rows, "ctx", axis=0, tiled=True),
        lax.all_gather(delta_rows, "ctx", axis=0, tiled=True),
    )
    own_keys = key_rows.reshape(row_count, head_count, HEAD)
    own_values = value_rows.reshape(row_count, head_count, HEAD)
    key_pos = own_first + local_pos
    empty_grad = jnp.zeros((row_count, head_count, HEAD), jnp.float32)
    query_piece = lax.all_gather(queries, "ctx", axis=0, tiled=True)
    d_piece = lax.all_gather(d_attn, "ctx", axis=0, tiled=True)
    piece_rows = query_piece.shape[0]

    def contribute(totals):
        query_heads = query_piece.reshape(piece_rows, head_count, HEAD)
        piece_heads = d_piece.reshape(piece_rows, head_count, HEAD)
        query_pos = jnp.arange(piece_rows, dtype=jnp.int32)
        lse_piece = lse_all.T
        delta_piece = delta_all.T
        scores = score_block(query_heads, own_keys, query_pos, key_pos)
        weights = jnp.exp(scores - lse_piece[:, :, None])
        d_probs = jnp.einsum(
            "rhe,khe->hrk", piece_heads, own_values, preferred_element_type=jnp.float32
        )
        d_scores = (weights * (d_probs - delta_piece[:, :, None])).astype(jnp.bfloat16)
        key_grad = jnp.einsum(
            "hrk,rhe->khe", d_scores, query_heads, preferred_element_type=jnp.float32
        )
        value_grad = jnp.einsum(
            "hrk,rhe->khe",
            weights.astype(jnp.bfloat16),
            piece_heads,
            preferred_element_type=jnp.float32,
        )
        return (key_grad, value_grad)

    def unchanged(totals):
        return totals

    key_grad, value_grad = lax.cond(
        jnp.int32(0) + piece_rows > own_first, contribute, unchanged, (empty_grad, empty_grad)
    )
    grad_keys = (key_grad * HEAD ** (-0.5)).reshape(row_count, channels).astype(jnp.bfloat16)
    grad_values = value_grad.reshape(row_count, channels).astype(jnp.bfloat16)
    return (
        mixed,
        grad_queries,
        grad_keys,
        grad_values,
        grad_gate_in,
        grad_gate_out,
        grad_filter,
        grad_gain,
    )


LOG2E = 1.4426950408889634
VMEM_LIMIT = 20 * 1024 * 1024
PACK_LIMIT = 54600 * 1024


def vmem_call(body, ins, outs, scratch=(), limit=VMEM_LIMIT, **extra):
    return pl.pallas_call(
        body,
        in_specs=ins,
        out_specs=tuple(spec for spec, _ in outs),
        out_shape=tuple(shape for _, shape in outs),
        scratch_shapes=list(scratch),
        compiler_params=pltpu.CompilerParams(vmem_limit_bytes=limit),
        **extra,
    )


def step(size, at):
    return [*range(0, size, 2), *range(1, size, 2)][at]


def set_apart(size):
    return range(size - size // 2 + 1, size)


def target(axis, at):
    size = lax.axis_size(axis)
    return lax.rem(lax.axis_index(axis) + step(size, at), size)


def origin(axis, at):
    size = lax.axis_size(axis)
    return lax.rem(lax.axis_index(axis) + size - step(size, at), size)


def start_all(copies):
    copies = list(copies)
    for copy in copies:
        copy.start()
    return copies


def wait_all(copies):
    for copy in copies:
        copy.wait()


def arrive(axis, pieces, held, tail=False):
    count = held.shape[1]
    for s, piece in enumerate(pieces):
        first = piece.shape[0] - count if tail else 0
        held[origin(axis, s)] = piece[first : first + count, :]


def depart(axis, held, pieces):
    for s, piece in enumerate(pieces):
        piece[...] = held[target(axis, s)]


def shift(piece, axis, by):
    size = lax.axis_size(axis)
    return lax.ppermute(piece, axis, [(i, (i + step(size, by)) % size) for i in range(size)])


def exchange(pieces, axis):
    size = lax.axis_size(axis)
    return [pieces[0]] + [shift(pieces[s], axis, s) for s in range(1, size)]


def dot_nt(a, b, precision=None):
    return lax.dot_general(
        a, b, (((1,), (1,)), ((), ())), precision=precision, preferred_element_type=jnp.float32
    )


def dot_nn(a, b):
    return lax.dot_general(a, b, (((1,), (0,)), ((), ())), preferred_element_type=jnp.float32)


def row_sums_as_lanes(product):
    ones = jnp.ones((8, product.shape[1]), jnp.float32)
    return dot_nt(ones, product, lax.Precision.HIGHEST)[0:1]


def channel_taps(taps_ref, head):
    groups = taps_ref.shape[1]
    size = HEAD * lax.axis_size("ctx") // groups
    wanted = head * (HEAD // size) + lax.broadcasted_iota(jnp.int32, (groups, HEAD), 1) // size
    spread = (wanted == lax.broadcasted_iota(jnp.int32, (groups, HEAD), 0)).astype(jnp.float32)
    return lax.dot_general(
        taps_ref[...],
        spread,
        (((1,), (0,)), ((), ())),
        precision=lax.Precision.HIGHEST,
        preferred_element_type=jnp.float32,
    )


def pack_body(axis, *refs):
    blocks = lax.axis_size(axis)
    arrays, refs = refs[:6], refs[6:]
    outs, apart, bufs, sems = refs[:blocks], refs[blocks:-7], refs[-7:-1], refs[-1]
    rows = arrays[0].shape[0]
    coming = start_all(
        pltpu.make_async_copy(ref, buf, sems.at[at]) for at, (ref, buf) in enumerate(zip(arrays, bufs))
    )
    gates = dict(zip(set_apart(blocks), apart))

    def store(at, s, block):
        if at >= 3 and s in gates:
            gates[s][(at - 3) * rows : (at - 2) * rows, :] = block
        else:
            outs[s][at * rows : (at + 1) * rows, :] = block

    columns = [pl.ds(pl.multiple_of(target(axis, s) * HEAD, HEAD), HEAD) for s in range(blocks)]
    for at in range(4):
        coming[at].wait()
        for s in range(blocks):
            store(at, s, bufs[at][:, columns[s]])
    wait_all(coming[4:])
    for s in range(blocks):
        d_conv = bufs[4][:, columns[s]].astype(jnp.float32) * bufs[5][:, columns[s]].astype(jnp.float32)
        store(4, s, d_conv.astype(jnp.bfloat16))


def coefficient_body(axis, token_ref, taps_ref, gain_ref, coef_ref):
    mine = lax.axis_index(axis)
    coef_ref[0:FILT, :] = channel_taps(taps_ref, mine)
    coef_ref[FILT : FILT + 1, :] = gain_ref[pl.ds(mine, 1), :]


def prepare_body(axis, token_ref, taps_ref, go_ref, ct_ref, wide_ref, dz_ref, du_pad):
    heads = lax.axis_size(axis)
    rows = go_ref.shape[0]
    du_pad[rows : rows + 8, :] = jnp.zeros((8, du_pad.shape[1]), jnp.float32)
    du_pad[0:rows, :] = go_ref[...].astype(jnp.float32) * ct_ref[...].astype(jnp.float32)
    for head in range(heads):
        cols = slice(head * HEAD, (head + 1) * HEAD)
        taps = channel_taps(taps_ref, head)
        wide_ref[0:FILT, cols] = taps
        dz = jnp.zeros((rows, HEAD), jnp.float32)
        for lag in range(FILT):
            dz = dz + taps[lag : lag + 1, :] * du_pad[lag : lag + rows, cols]
        dz_ref[:, cols] = dz


def attend_body(axis, *refs):
    blocks = lax.axis_size(axis)
    pieces, (p_ref, attn_ref, sq_ref, rx_ref) = refs[:blocks], refs[blocks:]
    arrive(axis, pieces, rx_ref)
    rows = rx_ref.shape[1] // 3
    tokens = blocks * rows
    wide = 2 * rows if blocks % 2 == 0 else rows
    per = wide // rows

    def part(at, first, count):
        return rx_ref[first : first + count, at * rows : (at + 1) * rows, :].reshape(count * rows, HEAD)

    v_t = part(2, 0, blocks).astype(jnp.float32).T.astype(jnp.bfloat16)
    scale = HEAD ** (-0.5) * LOG2E
    for i in range(tokens // wide):
        first, keys = i * wide, (i + 1) * wide
        s = dot_nt(part(1, 0, (i + 1) * per), part(0, i * per, per))
        key_pos = lax.broadcasted_iota(jnp.int32, (wide, wide), 0)
        query_pos = lax.broadcasted_iota(jnp.int32, (wide, wide), 1)
        edge = jnp.where(key_pos <= query_pos, s[first:], NEG)
        s = edge if i == 0 else jnp.concatenate([s[:first], edge], axis=0)
        top = jnp.max(s, axis=0, keepdims=True)
        e = jnp.exp2((s - top) * scale)
        p = (e * (1.0 / jnp.sum(e, axis=0, keepdims=True))).astype(jnp.bfloat16)
        p_ref[:keys, first:keys] = p
        attn_t = dot_nn(v_t[:, :keys], p).astype(jnp.bfloat16).astype(jnp.float32)
        squares = jnp.sum(attn_t * attn_t, axis=0, keepdims=True)
        for j in range(per):
            sq_ref[i * per + j : i * per + j + 1, :] = squares[:, j * rows : (j + 1) * rows]
        attn_ref[first:keys, :] = attn_t.T.astype(jnp.bfloat16)


def rowdot_body(axis, *refs):
    blocks = lax.axis_size(axis)
    pieces, refs = refs[:blocks], refs[blocks:]
    coef_ref, attn_ref, sq_ref, dz_ref, pay_ref, du_pad, sums, gate_ref = refs
    arrive(axis, pieces, gate_ref, tail=True)
    rows = gate_ref.shape[1] // 2
    tokens = blocks * rows
    for b in range(blocks):
        du_pad[b * rows : (b + 1) * rows, :] = gate_ref[b, rows:, :].astype(jnp.float32)
    du_pad[tokens : tokens + 8, :] = jnp.zeros((8, HEAD), jnp.float32)
    for b in range(blocks):
        first = b * rows
        dz = jnp.zeros((rows, HEAD), jnp.float32)
        for lag in range(FILT):
            dz = dz + coef_ref[lag : lag + 1, :] * du_pad[first + lag : first + lag + rows, :]
        dz_ref[first : first + rows, :] = dz
        scaled = dz * gate_ref[b, :rows, :].astype(jnp.float32) * coef_ref[FILT : FILT + 1, :]
        attn = attn_ref[first : first + rows, :].astype(jnp.float32)
        sums[blocks + b : blocks + b + 1, :] = row_sums_as_lanes(scaled * attn)
    sums[0:blocks, :] = sq_ref[...]
    low = sums[...].astype(jnp.bfloat16)
    for d in range(pay_ref.shape[0]):
        pay_ref[d] = low


def backward_body(axis, width, *refs):
    blocks = lax.axis_size(axis)
    pieces, gate_pieces, refs = refs[:blocks], refs[blocks : 2 * blocks], refs[2 * blocks :]
    rs_ref, coef_ref, p_ref, attn_ref, dz_ref = refs[:5]
    outs, (z_pad, ds_ref, da_ref, dl_ref, rx_ref, gate_ref, out_ref) = refs[5 : 5 + blocks], refs[5 + blocks :]
    arrive(axis, pieces, rx_ref)
    arrive(axis, gate_pieces, gate_ref, tail=True)
    rows = gate_ref.shape[1] // 2
    tokens = blocks * rows
    wide = 2 * rows if blocks % 2 == 0 else rows
    per = wide // rows
    gain = coef_ref[FILT : FILT + 1, :]

    def part(at, first, count):
        return rx_ref[first : first + count, at * rows : (at + 1) * rows, :].reshape(count * rows, HEAD)

    totals = jnp.sum(rs_ref[...].astype(jnp.float32), axis=0)
    rstd_lanes = 1.0 / jnp.sqrt(totals[:blocks] / width + EPS)
    pull_lanes = rstd_lanes * rstd_lanes * rstd_lanes * totals[blocks:] / width
    z_pad[0:8, :] = jnp.zeros((8, HEAD), jnp.float32)
    grads = [jnp.zeros((1, HEAD), jnp.float32) for _ in range(FILT + 1)]
    for b in range(blocks):
        first = b * rows
        rstd = jnp.broadcast_to(rstd_lanes[b : b + 1], (HEAD, rows)).T
        pull = jnp.broadcast_to(pull_lanes[b : b + 1], (HEAD, rows)).T
        attn = attn_ref[first : first + rows, :].astype(jnp.float32)
        dz = dz_ref[first : first + rows, :]
        gi = gate_ref[b, :rows, :].astype(jnp.float32)
        du = gate_ref[b, rows:, :].astype(jnp.float32)
        normed = attn * rstd * gain
        z_pad[8 + first : 8 + first + rows, :] = gi * normed
        for lag in range(FILT):
            z = z_pad[8 + first - lag : 8 + first - lag + rows, :]
            grads[lag] = grads[lag] + jnp.sum(du * z, axis=0, keepdims=True)
        out_ref[b, 3 * rows : 4 * rows, :] = normed.astype(jnp.bfloat16)
        edge = jnp.concatenate([z_pad[first : first + 8, :], dz[rows - 8 :]], axis=0)
        out_ref[b, 4 * rows : 4 * rows + 16, :] = edge.astype(jnp.bfloat16)
        d_normed = dz * gi
        grads[FILT] = grads[FILT] + jnp.sum(d_normed * attn * rstd, axis=0, keepdims=True)
        d_attn = (rstd * (d_normed * gain) - attn * pull).astype(jnp.bfloat16)
        da_ref[first : first + rows, :] = d_attn
        dl_ref[0:1, first : first + rows] = row_sums_as_lanes(d_attn.astype(jnp.float32) * attn)
    both = jnp.concatenate(grads, axis=0)
    high = both.astype(jnp.bfloat16).astype(jnp.float32)
    both = jnp.concatenate([high, both - high], axis=0).astype(jnp.bfloat16)
    for b in range(blocks):
        out_ref[b, 4 * rows + 16 : 4 * rows + 32, :] = both
    scale = HEAD ** (-0.5)
    k_t = part(1, 0, blocks).astype(jnp.float32).T.astype(jnp.bfloat16)
    for i in range(tokens // wide):
        first, keys = i * wide, (i + 1) * wide
        dp = dot_nt(part(2, 0, (i + 1) * per), da_ref[first : first + wide, :])
        p = p_ref[:keys, first : first + wide].astype(jnp.float32)
        ds = (p * (dp - dl_ref[0:1, first : first + wide])).astype(jnp.bfloat16)
        ds_ref[:keys, first : first + wide] = ds
        gq = (dot_nn(k_t[:, :keys], ds) * scale).T.astype(jnp.bfloat16)
        for j in range(per):
            out_ref[i * per + j, 0:rows, :] = gq[j * rows : (j + 1) * rows]
    for i in range(tokens // wide):
        first = i * wide
        q = part(0, i * per, blocks - i * per)
        gk = (dot_nn(ds_ref[first : first + wide, first:], q) * scale).astype(jnp.bfloat16)
        gv = dot_nn(p_ref[first : first + wide, first:], da_ref[first:, :]).astype(jnp.bfloat16)
        for j in range(per):
            out_ref[i * per + j, rows : 2 * rows, :] = gk[j * rows : (j + 1) * rows]
            out_ref[i * per + j, 2 * rows : 3 * rows, :] = gv[j * rows : (j + 1) * rows]
    depart(axis, out_ref, outs)


def unpack_body(axis, *refs):
    heads = lax.axis_size(axis)
    pieces, refs = refs[:heads], refs[heads:]
    gi_ref, go_ref, ct_ref, dz_ref, wide_ref = refs[:5]
    outs, (gf_ref, gg_ref), bufs, (z_pad, sems) = refs[5:11], refs[11:13], refs[13:19], refs[19:]
    rows = gi_ref.shape[0]
    leaving = [
        pltpu.make_async_copy(buf, ref, sems.at[at]) for at, (buf, ref) in enumerate(zip(bufs, outs))
    ]
    columns = [pl.ds(pl.multiple_of(origin(axis, s) * HEAD, HEAD), HEAD) for s in range(heads)]
    for at in range(3):
        for s, piece in enumerate(pieces):
            bufs[at][:, columns[s]] = piece[at * rows : (at + 1) * rows, :]
        leaving[at].start()
    for s, piece in enumerate(pieces):
        cols = columns[s]
        edge = piece[4 * rows : 4 * rows + 16, :].astype(jnp.float32)
        normed = piece[3 * rows : 4 * rows, :].astype(jnp.float32)
        z_pad[s, 0:8, :] = edge[0:8]
        z_pad[s, 8 : 8 + rows, :] = gi_ref[:, cols].astype(jnp.float32) * normed
        dz = jnp.concatenate([dz_ref[0 : rows - 8, cols], edge[8:16]], axis=0)
        bufs[3][:, cols] = (dz * normed).astype(jnp.bfloat16)
    leaving[3].start()
    for s in range(heads):
        cols = columns[s]
        conv = jnp.zeros((rows, HEAD), jnp.float32)
        for lag in range(FILT):
            conv = conv + wide_ref[lag : lag + 1, cols] * z_pad[s, 8 - lag : 8 - lag + rows, :]
        bufs[4][:, cols] = (go_ref[:, cols].astype(jnp.float32) * conv).astype(jnp.bfloat16)
        bufs[5][:, cols] = (ct_ref[:, cols].astype(jnp.float32) * conv).astype(jnp.bfloat16)
    leaving[4].start()
    leaving[5].start()
    groups = gf_ref.shape[1]
    size = HEAD * heads // groups
    channel = lax.broadcasted_iota(jnp.int32, (HEAD, groups), 0)
    group = lax.broadcasted_iota(jnp.int32, (HEAD, groups), 1)
    totals = jnp.zeros((16, groups), jnp.float32)
    for s, piece in enumerate(pieces):
        head = origin(axis, s)
        both = piece[4 * rows + 16 : 4 * rows + 32, :]
        gather = (head * (HEAD // size) + channel // size == group).astype(jnp.bfloat16)
        totals = totals + dot_nn(both, gather)
        total = both.astype(jnp.float32)
        gg_ref[pl.ds(head, 1), :] = total[FILT : FILT + 1] + total[8 + FILT : 8 + FILT + 1]
    gf_ref[...] = totals[:FILT] + totals[8 : 8 + FILT]
    wait_all(leaving)


def cost(flops, moved):
    return pl.CostEstimate(flops=flops, bytes_accessed=moved, transcendentals=0)


def shards_by_heads(
    queries, key_rows, value_rows, gate_in, gate_out, kernel_taps, norm_gain, cotangent
):
    rows, channels = queries.shape
    heads = channels // HEAD
    tokens = rows * heads
    everyone = lax.axis_size("ctx") * lax.axis_size("chan")
    low, full = jnp.bfloat16, jnp.float32
    near, far = pl.BlockSpec(memory_space=pltpu.VMEM), pl.BlockSpec(memory_space=pl.ANY)
    hbm = pl.BlockSpec(memory_space=pltpu.HBM)

    def here(shape, dtype):
        return near, jax.ShapeDtypeStruct(shape, dtype)

    def there(shape, dtype):
        return far, jax.ShapeDtypeStruct(shape, dtype)

    gain = norm_gain.reshape(heads, HEAD)
    taps = kernel_taps.T
    apart = set_apart(heads)
    flat = pltpu.VMEM((rows, channels), low)
    width = channels * lax.axis_size("chan")
    packed = vmem_call(
        functools.partial(pack_body, "ctx"),
        [hbm] * 6,
        [here(((3 if s in apart else 5) * rows, HEAD), low) for s in range(heads)]
        + [here((2 * rows, HEAD), low)] * len(apart),
        [flat] * 6 + [pltpu.SemaphoreType.DMA((6,))],
        limit=PACK_LIMIT,
    )(queries, key_rows, value_rows, gate_in, gate_out, cotangent)
    qkv = exchange(packed[:heads], "ctx")
    gates = list(qkv)
    for s, piece in zip(apart, packed[heads:]):
        gates[s] = shift(piece, "ctx", s)
    (coef,) = vmem_call(
        functools.partial(coefficient_body, "ctx"),
        [far] + [near] * 2,
        [here((8, HEAD), full)],
        cost_estimate=cost(rows * channels, rows * channels),
    )(packed[0], taps, gain)
    probs, attn, squares = vmem_call(
        functools.partial(attend_body, "ctx"),
        [near] * heads,
        [here((tokens, tokens), low), here((tokens, HEAD), low), here((heads, rows), full)],
        [pltpu.VMEM((heads, 3 * rows, HEAD), low)],
        cost_estimate=cost(4 * tokens * tokens * HEAD, 16 * tokens * tokens),
    )(*qkv)
    d_mixed, partial = vmem_call(
        functools.partial(rowdot_body, "ctx"),
        [near] * (heads + 3),
        [here((tokens, HEAD), full), here((everyone, 2 * heads, rows), low)],
        [
            pltpu.VMEM((tokens + 8, HEAD), full),
            pltpu.VMEM((2 * heads, rows), full),
            pltpu.VMEM((heads, 2 * rows, HEAD), low),
        ],
        cost_estimate=cost(rows * channels, rows * channels),
    )(*gates, coef, attn, squares)
    sums = lax.all_to_all(partial, ("ctx", "chan"), 0, 0, tiled=True)
    grads = vmem_call(
        functools.partial(backward_body, "ctx", width),
        [near] * (2 * heads + 5),
        [here((4 * rows + 32, HEAD), low)] * heads,
        [
            pltpu.VMEM((tokens + 8, HEAD), full),
            pltpu.VMEM((tokens, tokens), low),
            pltpu.VMEM((tokens, HEAD), low),
            pltpu.VMEM((8, tokens), full),
            pltpu.VMEM((heads, 3 * rows, HEAD), low),
            pltpu.VMEM((heads, 2 * rows, HEAD), low),
            pltpu.VMEM((heads, 4 * rows + 32, HEAD), low),
        ],
    )(*qkv, *gates, sums, coef, probs, attn, d_mixed)
    wide, own_d_mixed = vmem_call(
        functools.partial(prepare_body, "ctx"),
        [far] + [near] * 3,
        [here((8, channels), full), here((rows, channels), full)],
        [pltpu.VMEM((rows + 8, channels), full)],
        cost_estimate=cost(rows * channels * 20, rows * channels * 32),
    )(grads[0], taps, gate_out, cotangent)
    back = exchange(grads, "ctx")
    spread = (hbm, jax.ShapeDtypeStruct((rows, channels), low))
    gq, gk, gv, ggi, mixed, ggo, gf, gg = vmem_call(
        functools.partial(unpack_body, "ctx"),
        [near] * (heads + 5),
        [spread] * 6 + [here(kernel_taps.shape[::-1], full), here((heads, HEAD), full)],
        [flat] * 6 + [pltpu.VMEM((heads, rows + 8, HEAD), full), pltpu.SemaphoreType.DMA((6,))],
    )(*back, gate_in, gate_out, cotangent, own_d_mixed, wide)
    return (mixed, gq, gk, gv, ggi, ggo, gf.T, gg.reshape(channels))


def shards(queries, *rest):
    rows, channels = queries.shape
    by_heads = channels // HEAD == lax.axis_size("ctx") and rows == HEAD
    return (shards_by_heads if by_heads else shards_by_rows)(queries, *rest)


def solution(mesh):
    placed = (
        P("ctx", "chan"),
        P("ctx", "chan"),
        P("ctx", "chan"),
        P("ctx", "chan"),
        P("ctx", "chan"),
        P("chan", None),
        P("chan"),
        P("ctx", "chan"),
    )
    return jax.shard_map(
        shards,
        mesh=mesh,
        in_specs=placed,
        out_specs=(
            P("ctx", "chan"),
            P("ctx", "chan"),
            P("ctx", "chan"),
            P("ctx", "chan"),
            P("ctx", "chan"),
            P("ctx", "chan"),
            P("chan", None),
            P("chan"),
        ),
        check_vma=False,
    )
```

```python
import functools

import jax
import jax.numpy as jnp
from jax import lax
from jax.experimental import pallas as pl
from jax.experimental.pallas import tpu as pltpu
from jax.sharding import PartitionSpec as P

HEAD = 128
FILT = 7
WIDTH = 4096


EPS = 1e-06
NEG = -1e30


def from_behind(shard, axis, by):
    length = lax.axis_size(axis)
    pairs = [(i, i + by) for i in range(length) if 0 <= i + by < length]
    return lax.ppermute(shard, axis, pairs)


def score_block(query_heads, key_block, query_pos, key_pos):
    scores = jnp.einsum(
        "rhe,khe->hrk", query_heads, key_block, preferred_element_type=jnp.float32
    ) * HEAD ** (-0.5)
    allowed = query_pos[:, None] >= key_pos[None, :]
    return jnp.where(allowed[None], scores, NEG)


def row_totals(query_heads, query_pos, block_count, keys_heads, block_rows):
    row_count = query_heads.shape[0]
    head_count = query_heads.shape[1]

    def advance(block_index, running):
        row_max, row_sum = running
        first_key = block_index * block_rows
        key_block = lax.dynamic_slice_in_dim(keys_heads, first_key, block_rows, 0)
        key_pos = first_key + jnp.arange(block_rows, dtype=jnp.int32)
        scores = score_block(query_heads, key_block, query_pos, key_pos)
        new_max = jnp.maximum(row_max, jnp.max(scores, axis=2))
        row_sum = row_sum * jnp.exp(row_max - new_max) + jnp.sum(
            jnp.exp(scores - new_max[:, :, None]), axis=2
        )
        return (new_max, row_sum)

    initial = (
        jnp.full((head_count, row_count), NEG, jnp.float32),
        jnp.zeros((head_count, row_count), jnp.float32),
    )
    row_max, row_sum = lax.fori_loop(0, block_count, advance, initial)
    return row_max + jnp.log(row_sum)


def row_outputs(query_heads, query_pos, block_count, keys_heads, values_heads, lse, block_rows):
    row_count = query_heads.shape[0]
    head_count = query_heads.shape[1]

    def advance(block_index, summed):
        first_key = block_index * block_rows
        key_block = lax.dynamic_slice_in_dim(keys_heads, first_key, block_rows, 0)
        value_block = lax.dynamic_slice_in_dim(values_heads, first_key, block_rows, 0)
        key_pos = first_key + jnp.arange(block_rows, dtype=jnp.int32)
        scores = score_block(query_heads, key_block, query_pos, key_pos)
        weights_low = jnp.exp(scores - lse[:, :, None]).astype(jnp.bfloat16)
        return summed + jnp.einsum(
            "hrk,khe->rhe", weights_low, value_block, preferred_element_type=jnp.float32
        )

    summed = lax.fori_loop(
        0, block_count, advance, jnp.zeros((row_count, head_count, HEAD), jnp.float32)
    )
    return summed.reshape(row_count, head_count * HEAD).astype(jnp.bfloat16)


def query_grads(
    query_heads, d_heads, query_pos, block_count, keys_heads, values_heads, lse, delta, block_rows
):
    row_count = query_heads.shape[0]
    head_count = query_heads.shape[1]

    def advance(block_index, summed):
        first_key = block_index * block_rows
        key_block = lax.dynamic_slice_in_dim(keys_heads, first_key, block_rows, 0)
        value_block = lax.dynamic_slice_in_dim(values_heads, first_key, block_rows, 0)
        key_pos = first_key + jnp.arange(block_rows, dtype=jnp.int32)
        scores = score_block(query_heads, key_block, query_pos, key_pos)
        weights = jnp.exp(scores - lse[:, :, None])
        d_probs = jnp.einsum(
            "rhe,khe->hrk", d_heads, value_block, preferred_element_type=jnp.float32
        )
        d_scores = (weights * (d_probs - delta[:, :, None])).astype(jnp.bfloat16)
        return summed + jnp.einsum(
            "hrk,khe->rhe", d_scores, key_block, preferred_element_type=jnp.float32
        )

    summed = lax.fori_loop(
        0, block_count, advance, jnp.zeros((row_count, head_count, HEAD), jnp.float32)
    )
    return (summed * HEAD ** (-0.5)).reshape(row_count, head_count * HEAD).astype(jnp.bfloat16)


def shards_by_rows(queries, key_rows, value_rows, gate_in, gate_out, kernel_taps, norm_gain, cotangent):
    row_count = queries.shape[0]
    channels = queries.shape[1]
    head_count = channels // HEAD
    group_count = kernel_taps.shape[0]
    devices = lax.axis_size("ctx")
    position = lax.axis_index("ctx")
    own_first = position * row_count
    total_rows = row_count * devices
    block_rows = min(512, total_rows)
    local_pos = jnp.arange(row_count, dtype=jnp.int32)
    keys_all, values_all = (
        lax.all_gather(key_rows, "ctx", axis=0, tiled=True),
        lax.all_gather(value_rows, "ctx", axis=0, tiled=True),
    )
    keys_heads = keys_all.reshape(total_rows, head_count, HEAD)
    query_sets = (queries, own_first + local_pos)
    query_block, query_pos = query_sets
    block_count = query_pos[-1] // block_rows + 1
    lse_sets = row_totals(
        query_block.reshape(-1, head_count, HEAD), query_pos, block_count, keys_heads, block_rows
    )
    values_heads = values_all.reshape(total_rows, head_count, HEAD)
    query_block, query_pos = query_sets
    outputs = row_outputs(
        query_block.reshape(-1, head_count, HEAD),
        query_pos,
        block_count,
        keys_heads,
        values_heads,
        lse_sets,
        block_rows,
    )
    lse_rows = lse_sets.T
    attn_wide = outputs.astype(jnp.float32)
    square_sum = lax.psum(jnp.sum(attn_wide * attn_wide, axis=1), "chan")
    inverse_rms = 1.0 / jnp.sqrt(square_sum / WIDTH + EPS)
    normed = attn_wide * inverse_rms[:, None] * norm_gain[None, :]
    gate_wide = gate_in.astype(jnp.float32)
    mixed_in = gate_wide * normed
    taps = jnp.broadcast_to(
        kernel_taps[:, None, :], (group_count, channels // group_count, FILT)
    ).reshape(channels, FILT)
    rim_before = from_behind(mixed_in[row_count - (FILT - 1) :], "ctx", 1)
    extended = jnp.concatenate([rim_before, mixed_in], axis=0)
    conv_out = jnp.zeros((row_count, channels), jnp.float32)
    for lag in range(FILT):
        conv_out = (
            conv_out + taps[:, lag][None, :] * extended[FILT - 1 - lag : FILT - 1 - lag + row_count]
        )
    out_gate = gate_out.astype(jnp.float32)
    mixed = (out_gate * conv_out).astype(jnp.bfloat16)
    upstream = cotangent.astype(jnp.float32)
    grad_gate_out = (upstream * conv_out).astype(jnp.bfloat16)
    d_conv = upstream * out_gate
    tap_columns = []
    for lag in range(FILT):
        per_channel = jnp.sum(
            d_conv * extended[FILT - 1 - lag : FILT - 1 - lag + row_count], axis=0
        )
        tap_columns.append(per_channel.reshape(group_count, -1).sum(axis=1))
    tap_terms = jnp.stack(tap_columns, axis=1)
    rim_after = from_behind(d_conv[: FILT - 1], "ctx", -1)
    extended_grad = jnp.concatenate([d_conv, rim_after], axis=0)
    d_mixed = jnp.zeros((row_count, channels), jnp.float32)
    for lag in range(FILT):
        d_mixed = d_mixed + taps[:, lag][None, :] * extended_grad[lag : lag + row_count]
    grad_gate_in = (d_mixed * normed).astype(jnp.bfloat16)
    d_normed = d_mixed * gate_wide
    gain_terms = jnp.sum(d_normed * attn_wide * inverse_rms[:, None], axis=0)
    grad_filter, grad_gain = lax.psum((tap_terms, gain_terms), "ctx")
    scaled = d_normed * norm_gain[None, :]
    row_dot = lax.psum(jnp.sum(scaled * attn_wide, axis=1), "chan")
    d_attn = (
        inverse_rms[:, None] * scaled - attn_wide * (inverse_rms**3 * row_dot / WIDTH)[:, None]
    ).astype(jnp.bfloat16)
    d_heads = d_attn.reshape(row_count, head_count, HEAD)
    delta_rows = jnp.sum(
        d_heads.astype(jnp.float32) * attn_wide.reshape(row_count, head_count, HEAD), axis=2
    )
    own_count = (own_first + row_count - 1) // block_rows + 1
    grad_queries = query_grads(
        queries.reshape(row_count, head_count, HEAD),
        d_heads,
        own_first + local_pos,
        own_count,
        keys_heads,
        values_heads,
        lse_rows.T,
        delta_rows.T,
        block_rows,
    )
    lse_all, delta_all = (
        lax.all_gather(lse_rows, "ctx", axis=0, tiled=True),
        lax.all_gather(delta_rows, "ctx", axis=0, tiled=True),
    )
    own_keys = key_rows.reshape(row_count, head_count, HEAD)
    own_values = value_rows.reshape(row_count, head_count, HEAD)
    key_pos = own_first + local_pos
    empty_grad = jnp.zeros((row_count, head_count, HEAD), jnp.float32)
    query_piece = lax.all_gather(queries, "ctx", axis=0, tiled=True)
    d_piece = lax.all_gather(d_attn, "ctx", axis=0, tiled=True)
    piece_rows = query_piece.shape[0]

    def contribute(totals):
        query_heads = query_piece.reshape(piece_rows, head_count, HEAD)
        piece_heads = d_piece.reshape(piece_rows, head_count, HEAD)
        query_pos = jnp.arange(piece_rows, dtype=jnp.int32)
        lse_piece = lse_all.T
        delta_piece = delta_all.T
        scores = score_block(query_heads, own_keys, query_pos, key_pos)
        weights = jnp.exp(scores - lse_piece[:, :, None])
        d_probs = jnp.einsum(
            "rhe,khe->hrk", piece_heads, own_values, preferred_element_type=jnp.float32
        )
        d_scores = (weights * (d_probs - delta_piece[:, :, None])).astype(jnp.bfloat16)
        key_grad = jnp.einsum(
            "hrk,rhe->khe", d_scores, query_heads, preferred_element_type=jnp.float32
        )
        value_grad = jnp.einsum(
            "hrk,rhe->khe",
            weights.astype(jnp.bfloat16),
            piece_heads,
            preferred_element_type=jnp.float32,
        )
        return (key_grad, value_grad)

    def unchanged(totals):
        return totals

    key_grad, value_grad = lax.cond(
        jnp.int32(0) + piece_rows > own_first, contribute, unchanged, (empty_grad, empty_grad)
    )
    grad_keys = (key_grad * HEAD ** (-0.5)).reshape(row_count, channels).astype(jnp.bfloat16)
    grad_values = value_grad.reshape(row_count, channels).astype(jnp.bfloat16)
    return (
        mixed,
        grad_queries,
        grad_keys,
        grad_values,
        grad_gate_in,
        grad_gate_out,
        grad_filter,
        grad_gain,
    )


LOG2E = 1.4426950408889634
VMEM_LIMIT = 20 * 1024 * 1024
PACK_LIMIT = 54400 * 1024


def vmem_call(body, ins, outs, scratch=(), limit=VMEM_LIMIT, **extra):
    return pl.pallas_call(
        body,
        in_specs=ins,
        out_specs=tuple(spec for spec, _ in outs),
        out_shape=tuple(shape for _, shape in outs),
        scratch_shapes=list(scratch),
        compiler_params=pltpu.CompilerParams(vmem_limit_bytes=limit),
        **extra,
    )


def step(size, at):
    return [*range(0, size, 2), *range(1, size, 2)][at]


def set_apart(size):
    return range(size - size // 2 + 1, size)


def target(axis, at):
    size = lax.axis_size(axis)
    return lax.rem(lax.axis_index(axis) + step(size, at), size)


def origin(axis, at):
    size = lax.axis_size(axis)
    return lax.rem(lax.axis_index(axis) + size - step(size, at), size)


def start_all(copies):
    copies = list(copies)
    for copy in copies:
        copy.start()
    return copies


def wait_all(copies):
    for copy in copies:
        copy.wait()


def arrive(axis, pieces, held, tail=False):
    count = held.shape[1]
    for s, piece in enumerate(pieces):
        first = piece.shape[0] - count if tail else 0
        held[origin(axis, s)] = piece[first : first + count, :]


def depart(axis, held, pieces):
    for s, piece in enumerate(pieces):
        piece[...] = held[target(axis, s)]


def shift(piece, axis, by):
    size = lax.axis_size(axis)
    return lax.ppermute(piece, axis, [(i, (i + step(size, by)) % size) for i in range(size)])


def exchange(pieces, axis):
    size = lax.axis_size(axis)
    return [pieces[0]] + [shift(pieces[s], axis, s) for s in range(1, size)]


def dot_nt(a, b, precision=None):
    return lax.dot_general(
        a, b, (((1,), (1,)), ((), ())), precision=precision, preferred_element_type=jnp.float32
    )


def dot_nn(a, b):
    return lax.dot_general(a, b, (((1,), (0,)), ((), ())), preferred_element_type=jnp.float32)


def row_sums_as_lanes(product):
    ones = jnp.ones((8, product.shape[1]), jnp.bfloat16)
    high = product.astype(jnp.bfloat16)
    rest = (product - high.astype(jnp.float32)).astype(jnp.bfloat16)
    return (dot_nt(ones, high) + dot_nt(ones, rest))[0:1]


def channel_taps(taps_ref, head):
    groups = taps_ref.shape[1]
    size = HEAD * lax.axis_size("ctx") // groups
    wanted = head * (HEAD // size) + lax.broadcasted_iota(jnp.int32, (groups, HEAD), 1) // size
    spread = (wanted == lax.broadcasted_iota(jnp.int32, (groups, HEAD), 0)).astype(jnp.float32)
    return lax.dot_general(
        taps_ref[...],
        spread,
        (((1,), (0,)), ((), ())),
        precision=lax.Precision.HIGHEST,
        preferred_element_type=jnp.float32,
    )


def pack_body(axis, *refs):
    blocks = lax.axis_size(axis)
    arrays, refs = refs[:6], refs[6:]
    outs, apart, bufs, sems = refs[:blocks], refs[blocks:-7], refs[-7:-1], refs[-1]
    rows = arrays[0].shape[0]
    coming = start_all(
        pltpu.make_async_copy(ref, buf, sems.at[at]) for at, (ref, buf) in enumerate(zip(arrays, bufs))
    )
    gates = dict(zip(set_apart(blocks), apart))

    def store(at, s, block):
        if at >= 3 and s in gates:
            gates[s][(at - 3) * rows : (at - 2) * rows, :] = block
        else:
            outs[s][at * rows : (at + 1) * rows, :] = block

    columns = [pl.ds(pl.multiple_of(target(axis, s) * HEAD, HEAD), HEAD) for s in range(blocks)]
    for at in range(4):
        coming[at].wait()
        for s in range(blocks):
            store(at, s, bufs[at][:, columns[s]])
    wait_all(coming[4:])
    for s in range(blocks):
        d_conv = bufs[4][:, columns[s]].astype(jnp.float32) * bufs[5][:, columns[s]].astype(jnp.float32)
        store(4, s, d_conv.astype(jnp.bfloat16))


def coefficient_body(axis, token_ref, taps_ref, gain_ref, coef_ref):
    mine = lax.axis_index(axis)
    coef_ref[0:FILT, :] = channel_taps(taps_ref, mine)
    coef_ref[FILT : FILT + 1, :] = gain_ref[pl.ds(mine, 1), :]


def prepare_body(axis, token_ref, taps_ref, go_ref, ct_ref, wide_ref, dz_ref, du_pad):
    heads = lax.axis_size(axis)
    rows = go_ref.shape[0]
    du_pad[rows : rows + 8, :] = jnp.zeros((8, du_pad.shape[1]), jnp.float32)
    du_pad[0:rows, :] = go_ref[...].astype(jnp.float32) * ct_ref[...].astype(jnp.float32)
    for head in range(heads):
        cols = slice(head * HEAD, (head + 1) * HEAD)
        taps = channel_taps(taps_ref, head)
        wide_ref[0:FILT, cols] = taps
        dz = jnp.zeros((rows, HEAD), jnp.float32)
        for lag in range(FILT):
            dz = dz + taps[lag : lag + 1, :] * du_pad[lag : lag + rows, cols]
        dz_ref[:, cols] = dz


def attend_body(axis, *refs):
    blocks = lax.axis_size(axis)
    pieces, (p_ref, attn_ref, sq_ref, rx_ref) = refs[:blocks], refs[blocks:]
    arrive(axis, pieces, rx_ref)
    rows = rx_ref.shape[1] // 3
    tokens = blocks * rows
    wide = 2 * rows if blocks % 2 == 0 else rows
    per = wide // rows

    def part(at, first, count):
        return rx_ref[first : first + count, at * rows : (at + 1) * rows, :].reshape(count * rows, HEAD)

    v_t = part(2, 0, blocks).astype(jnp.float32).T.astype(jnp.bfloat16)
    scale = HEAD ** (-0.5) * LOG2E
    for i in range(tokens // wide):
        first, keys = i * wide, (i + 1) * wide
        s = dot_nt(part(1, 0, (i + 1) * per), part(0, i * per, per))
        key_pos = lax.broadcasted_iota(jnp.int32, (wide, wide), 0)
        query_pos = lax.broadcasted_iota(jnp.int32, (wide, wide), 1)
        edge = jnp.where(key_pos <= query_pos, s[first:], NEG)
        s = edge if i == 0 else jnp.concatenate([s[:first], edge], axis=0)
        top = jnp.max(s, axis=0, keepdims=True)
        e = jnp.exp2((s - top) * scale)
        p = (e * (1.0 / jnp.sum(e, axis=0, keepdims=True))).astype(jnp.bfloat16)
        p_ref[:keys, first:keys] = p
        attn_t = dot_nn(v_t[:, :keys], p).astype(jnp.bfloat16).astype(jnp.float32)
        squares = jnp.sum(attn_t * attn_t, axis=0, keepdims=True)
        for j in range(per):
            sq_ref[i * per + j : i * per + j + 1, :] = squares[:, j * rows : (j + 1) * rows]
        attn_ref[first:keys, :] = attn_t.T.astype(jnp.bfloat16)


def rowdot_body(axis, *refs):
    blocks = lax.axis_size(axis)
    pieces, refs = refs[:blocks], refs[blocks:]
    coef_ref, attn_ref, sq_ref, dz_ref, pay_ref, du_pad, sums, gate_ref = refs
    arrive(axis, pieces, gate_ref, tail=True)
    rows = gate_ref.shape[1] // 2
    tokens = blocks * rows
    for b in range(blocks):
        du_pad[b * rows : (b + 1) * rows, :] = gate_ref[b, rows:, :].astype(jnp.float32)
    du_pad[tokens : tokens + 8, :] = jnp.zeros((8, HEAD), jnp.float32)
    for b in range(blocks):
        first = b * rows
        dz = jnp.zeros((rows, HEAD), jnp.float32)
        for lag in range(FILT):
            dz = dz + coef_ref[lag : lag + 1, :] * du_pad[first + lag : first + lag + rows, :]
        dz_ref[first : first + rows, :] = dz
        scaled = dz * gate_ref[b, :rows, :].astype(jnp.float32) * coef_ref[FILT : FILT + 1, :]
        attn = attn_ref[first : first + rows, :].astype(jnp.float32)
        sums[blocks + b : blocks + b + 1, :] = row_sums_as_lanes(scaled * attn)
    sums[0:blocks, :] = sq_ref[...]
    low = sums[...].astype(jnp.bfloat16)
    for d in range(pay_ref.shape[0]):
        pay_ref[d] = low


def backward_body(axis, width, *refs):
    blocks = lax.axis_size(axis)
    pieces, gate_pieces, refs = refs[:blocks], refs[blocks : 2 * blocks], refs[2 * blocks :]
    rs_ref, coef_ref, p_ref, attn_ref, dz_ref = refs[:5]
    outs, (z_pad, ds_ref, da_ref, dl_ref, rx_ref, gate_ref, out_ref) = refs[5 : 5 + blocks], refs[5 + blocks :]
    arrive(axis, pieces, rx_ref)
    arrive(axis, gate_pieces, gate_ref, tail=True)
    rows = gate_ref.shape[1] // 2
    tokens = blocks * rows
    wide = 2 * rows if blocks % 2 == 0 else rows
    per = wide // rows
    gain = coef_ref[FILT : FILT + 1, :]

    def part(at, first, count):
        return rx_ref[first : first + count, at * rows : (at + 1) * rows, :].reshape(count * rows, HEAD)

    totals = jnp.sum(rs_ref[...].astype(jnp.float32), axis=0)
    rstd_lanes = 1.0 / jnp.sqrt(totals[:blocks] / width + EPS)
    pull_lanes = rstd_lanes * rstd_lanes * rstd_lanes * totals[blocks:] / width
    z_pad[0:8, :] = jnp.zeros((8, HEAD), jnp.float32)
    grads = [jnp.zeros((1, HEAD), jnp.float32) for _ in range(FILT + 1)]
    for b in range(blocks):
        first = b * rows
        rstd = jnp.broadcast_to(rstd_lanes[b : b + 1], (HEAD, rows)).T
        pull = jnp.broadcast_to(pull_lanes[b : b + 1], (HEAD, rows)).T
        attn = attn_ref[first : first + rows, :].astype(jnp.float32)
        dz = dz_ref[first : first + rows, :]
        gi = gate_ref[b, :rows, :].astype(jnp.float32)
        du = gate_ref[b, rows:, :].astype(jnp.float32)
        normed = attn * rstd * gain
        z_pad[8 + first : 8 + first + rows, :] = gi * normed
        for lag in range(FILT):
            z = z_pad[8 + first - lag : 8 + first - lag + rows, :]
            grads[lag] = grads[lag] + jnp.sum(du * z, axis=0, keepdims=True)
        out_ref[b, 3 * rows : 4 * rows, :] = normed.astype(jnp.bfloat16)
        edge = jnp.concatenate([z_pad[first : first + 8, :], dz[rows - 8 :]], axis=0)
        out_ref[b, 4 * rows : 4 * rows + 16, :] = edge.astype(jnp.bfloat16)
        d_normed = dz * gi
        grads[FILT] = grads[FILT] + jnp.sum(d_normed * attn * rstd, axis=0, keepdims=True)
        d_attn = (rstd * (d_normed * gain) - attn * pull).astype(jnp.bfloat16)
        da_ref[first : first + rows, :] = d_attn
        dl_ref[0:1, first : first + rows] = row_sums_as_lanes(d_attn.astype(jnp.float32) * attn)
    both = jnp.concatenate(grads, axis=0)
    high = both.astype(jnp.bfloat16).astype(jnp.float32)
    both = jnp.concatenate([high, both - high], axis=0).astype(jnp.bfloat16)
    for b in range(blocks):
        out_ref[b, 4 * rows + 16 : 4 * rows + 32, :] = both
    scale = HEAD ** (-0.5)
    k_t = part(1, 0, blocks).astype(jnp.float32).T.astype(jnp.bfloat16)
    for i in range(tokens // wide):
        first, keys = i * wide, (i + 1) * wide
        dp = dot_nt(part(2, 0, (i + 1) * per), da_ref[first : first + wide, :])
        p = p_ref[:keys, first : first + wide].astype(jnp.float32)
        ds = (p * (dp - dl_ref[0:1, first : first + wide])).astype(jnp.bfloat16)
        ds_ref[:keys, first : first + wide] = ds
        gq = (dot_nn(k_t[:, :keys], ds) * scale).T.astype(jnp.bfloat16)
        for j in range(per):
            out_ref[i * per + j, 0:rows, :] = gq[j * rows : (j + 1) * rows]
    for i in range(tokens // wide):
        first = i * wide
        q = part(0, i * per, blocks - i * per)
        gk = (dot_nn(ds_ref[first : first + wide, first:], q) * scale).astype(jnp.bfloat16)
        gv = dot_nn(p_ref[first : first + wide, first:], da_ref[first:, :]).astype(jnp.bfloat16)
        for j in range(per):
            out_ref[i * per + j, rows : 2 * rows, :] = gk[j * rows : (j + 1) * rows]
            out_ref[i * per + j, 2 * rows : 3 * rows, :] = gv[j * rows : (j + 1) * rows]
    depart(axis, out_ref, outs)


def unpack_body(axis, *refs):
    heads = lax.axis_size(axis)
    pieces, refs = refs[:heads], refs[heads:]
    gi_ref, go_ref, ct_ref, dz_ref, wide_ref = refs[:5]
    outs, (gf_ref, gg_ref), bufs, (z_pad, sems) = refs[5:11], refs[11:13], refs[13:19], refs[19:]
    rows = gi_ref.shape[0]
    leaving = [
        pltpu.make_async_copy(buf, ref, sems.at[at]) for at, (buf, ref) in enumerate(zip(bufs, outs))
    ]
    columns = [pl.ds(pl.multiple_of(origin(axis, s) * HEAD, HEAD), HEAD) for s in range(heads)]
    for at in range(3):
        for s, piece in enumerate(pieces):
            bufs[at][:, columns[s]] = piece[at * rows : (at + 1) * rows, :]
        leaving[at].start()
    for s, piece in enumerate(pieces):
        cols = columns[s]
        edge = piece[4 * rows : 4 * rows + 16, :].astype(jnp.float32)
        normed = piece[3 * rows : 4 * rows, :].astype(jnp.float32)
        z_pad[s, 0:8, :] = edge[0:8]
        z_pad[s, 8 : 8 + rows, :] = gi_ref[:, cols].astype(jnp.float32) * normed
        dz = jnp.concatenate([dz_ref[0 : rows - 8, cols], edge[8:16]], axis=0)
        bufs[3][:, cols] = (dz * normed).astype(jnp.bfloat16)
    leaving[3].start()
    for s in range(heads):
        cols = columns[s]
        conv = jnp.zeros((rows, HEAD), jnp.float32)
        for lag in range(FILT):
            conv = conv + wide_ref[lag : lag + 1, cols] * z_pad[s, 8 - lag : 8 - lag + rows, :]
        bufs[4][:, cols] = (go_ref[:, cols].astype(jnp.float32) * conv).astype(jnp.bfloat16)
        bufs[5][:, cols] = (ct_ref[:, cols].astype(jnp.float32) * conv).astype(jnp.bfloat16)
    leaving[4].start()
    leaving[5].start()
    groups = gf_ref.shape[1]
    size = HEAD * heads // groups
    channel = lax.broadcasted_iota(jnp.int32, (HEAD, groups), 0)
    group = lax.broadcasted_iota(jnp.int32, (HEAD, groups), 1)
    totals = jnp.zeros((16, groups), jnp.float32)
    for s, piece in enumerate(pieces):
        head = origin(axis, s)
        both = piece[4 * rows + 16 : 4 * rows + 32, :]
        gather = (head * (HEAD // size) + channel // size == group).astype(jnp.bfloat16)
        totals = totals + dot_nn(both, gather)
        total = both.astype(jnp.float32)
        gg_ref[pl.ds(head, 1), :] = total[FILT : FILT + 1] + total[8 + FILT : 8 + FILT + 1]
    gf_ref[...] = totals[:FILT] + totals[8 : 8 + FILT]
    wait_all(leaving)


def cost(flops, moved):
    return pl.CostEstimate(flops=flops, bytes_accessed=moved, transcendentals=0)


def shards_by_heads(
    queries, key_rows, value_rows, gate_in, gate_out, kernel_taps, norm_gain, cotangent
):
    rows, channels = queries.shape
    heads = channels // HEAD
    tokens = rows * heads
    everyone = lax.axis_size("ctx") * lax.axis_size("chan")
    low, full = jnp.bfloat16, jnp.float32
    near, far = pl.BlockSpec(memory_space=pltpu.VMEM), pl.BlockSpec(memory_space=pl.ANY)
    hbm = pl.BlockSpec(memory_space=pltpu.HBM)

    def here(shape, dtype):
        return near, jax.ShapeDtypeStruct(shape, dtype)

    def there(shape, dtype):
        return far, jax.ShapeDtypeStruct(shape, dtype)

    gain = norm_gain.reshape(heads, HEAD)
    taps = kernel_taps.T
    apart = set_apart(heads)
    flat = pltpu.VMEM((rows, channels), low)
    width = channels * lax.axis_size("chan")
    packed = vmem_call(
        functools.partial(pack_body, "ctx"),
        [hbm] * 6,
        [here(((3 if s in apart else 5) * rows, HEAD), low) for s in range(heads)]
        + [here((2 * rows, HEAD), low)] * len(apart),
        [flat] * 6 + [pltpu.SemaphoreType.DMA((6,))],
        limit=PACK_LIMIT,
    )(queries, key_rows, value_rows, gate_in, gate_out, cotangent)
    qkv = exchange(packed[:heads], "ctx")
    gates = list(qkv)
    for s, piece in zip(apart, packed[heads:]):
        gates[s] = shift(piece, "ctx", s)
    (coef,) = vmem_call(
        functools.partial(coefficient_body, "ctx"),
        [far] + [near] * 2,
        [here((8, HEAD), full)],
        cost_estimate=cost(rows * channels, rows * channels),
    )(packed[0], taps, gain)
    probs, attn, squares = vmem_call(
        functools.partial(attend_body, "ctx"),
        [near] * heads,
        [here((tokens, tokens), low), here((tokens, HEAD), low), here((heads, rows), full)],
        [pltpu.VMEM((heads, 3 * rows, HEAD), low)],
        cost_estimate=cost(4 * tokens * tokens * HEAD, 16 * tokens * tokens),
    )(*qkv)
    d_mixed, partial = vmem_call(
        functools.partial(rowdot_body, "ctx"),
        [near] * (heads + 3),
        [here((tokens, HEAD), full), here((everyone, 2 * heads, rows), low)],
        [
            pltpu.VMEM((tokens + 8, HEAD), full),
            pltpu.VMEM((2 * heads, rows), full),
            pltpu.VMEM((heads, 2 * rows, HEAD), low),
        ],
        cost_estimate=cost(rows * channels, rows * channels),
    )(*gates, coef, attn, squares)
    sums = lax.all_to_all(partial, ("ctx", "chan"), 0, 0, tiled=True)
    grads = vmem_call(
        functools.partial(backward_body, "ctx", width),
        [near] * (2 * heads + 5),
        [here((4 * rows + 32, HEAD), low)] * heads,
        [
            pltpu.VMEM((tokens + 8, HEAD), full),
            pltpu.VMEM((tokens, tokens), low),
            pltpu.VMEM((tokens, HEAD), low),
            pltpu.VMEM((8, tokens), full),
            pltpu.VMEM((heads, 3 * rows, HEAD), low),
            pltpu.VMEM((heads, 2 * rows, HEAD), low),
            pltpu.VMEM((heads, 4 * rows + 32, HEAD), low),
        ],
    )(*qkv, *gates, sums, coef, probs, attn, d_mixed)
    wide, own_d_mixed = vmem_call(
        functools.partial(prepare_body, "ctx"),
        [far] + [near] * 3,
        [here((8, channels), full), here((rows, channels), full)],
        [pltpu.VMEM((rows + 8, channels), full)],
        cost_estimate=cost(rows * channels * 20, rows * channels * 32),
    )(grads[0], taps, gate_out, cotangent)
    back = exchange(grads, "ctx")
    spread = (hbm, jax.ShapeDtypeStruct((rows, channels), low))
    gq, gk, gv, ggi, mixed, ggo, gf, gg = vmem_call(
        functools.partial(unpack_body, "ctx"),
        [near] * (heads + 5),
        [spread] * 6 + [here(kernel_taps.shape[::-1], full), here((heads, HEAD), full)],
        [flat] * 6 + [pltpu.VMEM((heads, rows + 8, HEAD), full), pltpu.SemaphoreType.DMA((6,))],
    )(*back, gate_in, gate_out, cotangent, own_d_mixed, wide)
    return (mixed, gq, gk, gv, ggi, ggo, gf.T, gg.reshape(channels))


def shards(queries, *rest):
    rows, channels = queries.shape
    by_heads = channels // HEAD == lax.axis_size("ctx") and rows == HEAD
    return (shards_by_heads if by_heads else shards_by_rows)(queries, *rest)


def solution(mesh):
    placed = (
        P("ctx", "chan"),
        P("ctx", "chan"),
        P("ctx", "chan"),
        P("ctx", "chan"),
        P("ctx", "chan"),
        P("chan", None),
        P("chan"),
        P("ctx", "chan"),
    )
    return jax.shard_map(
        shards,
        mesh=mesh,
        in_specs=placed,
        out_specs=(
            P("ctx", "chan"),
            P("ctx", "chan"),
            P("ctx", "chan"),
            P("ctx", "chan"),
            P("ctx", "chan"),
            P("ctx", "chan"),
            P("chan", None),
            P("chan"),
        ),
        check_vma=False,
    )
```

```python
import functools

import jax
import jax.numpy as jnp
from jax import lax
from jax.experimental import pallas as pl
from jax.experimental.pallas import tpu as pltpu
from jax.sharding import PartitionSpec as P

HEAD = 128
FILT = 7
WIDTH = 4096


EPS = 1e-06
NEG = -1e30


def from_behind(shard, axis, by):
    length = lax.axis_size(axis)
    pairs = [(i, i + by) for i in range(length) if 0 <= i + by < length]
    return lax.ppermute(shard, axis, pairs)


def score_block(query_heads, key_block, query_pos, key_pos):
    scores = jnp.einsum(
        "rhe,khe->hrk", query_heads, key_block, preferred_element_type=jnp.float32
    ) * HEAD ** (-0.5)
    allowed = query_pos[:, None] >= key_pos[None, :]
    return jnp.where(allowed[None], scores, NEG)


def row_totals(query_heads, query_pos, block_count, keys_heads, block_rows):
    row_count = query_heads.shape[0]
    head_count = query_heads.shape[1]

    def advance(block_index, running):
        row_max, row_sum = running
        first_key = block_index * block_rows
        key_block = lax.dynamic_slice_in_dim(keys_heads, first_key, block_rows, 0)
        key_pos = first_key + jnp.arange(block_rows, dtype=jnp.int32)
        scores = score_block(query_heads, key_block, query_pos, key_pos)
        new_max = jnp.maximum(row_max, jnp.max(scores, axis=2))
        row_sum = row_sum * jnp.exp(row_max - new_max) + jnp.sum(
            jnp.exp(scores - new_max[:, :, None]), axis=2
        )
        return (new_max, row_sum)

    initial = (
        jnp.full((head_count, row_count), NEG, jnp.float32),
        jnp.zeros((head_count, row_count), jnp.float32),
    )
    row_max, row_sum = lax.fori_loop(0, block_count, advance, initial)
    return row_max + jnp.log(row_sum)


def row_outputs(query_heads, query_pos, block_count, keys_heads, values_heads, lse, block_rows):
    row_count = query_heads.shape[0]
    head_count = query_heads.shape[1]

    def advance(block_index, summed):
        first_key = block_index * block_rows
        key_block = lax.dynamic_slice_in_dim(keys_heads, first_key, block_rows, 0)
        value_block = lax.dynamic_slice_in_dim(values_heads, first_key, block_rows, 0)
        key_pos = first_key + jnp.arange(block_rows, dtype=jnp.int32)
        scores = score_block(query_heads, key_block, query_pos, key_pos)
        weights_low = jnp.exp(scores - lse[:, :, None]).astype(jnp.bfloat16)
        return summed + jnp.einsum(
            "hrk,khe->rhe", weights_low, value_block, preferred_element_type=jnp.float32
        )

    summed = lax.fori_loop(
        0, block_count, advance, jnp.zeros((row_count, head_count, HEAD), jnp.float32)
    )
    return summed.reshape(row_count, head_count * HEAD).astype(jnp.bfloat16)


def query_grads(
    query_heads, d_heads, query_pos, block_count, keys_heads, values_heads, lse, delta, block_rows
):
    row_count = query_heads.shape[0]
    head_count = query_heads.shape[1]

    def advance(block_index, summed):
        first_key = block_index * block_rows
        key_block = lax.dynamic_slice_in_dim(keys_heads, first_key, block_rows, 0)
        value_block = lax.dynamic_slice_in_dim(values_heads, first_key, block_rows, 0)
        key_pos = first_key + jnp.arange(block_rows, dtype=jnp.int32)
        scores = score_block(query_heads, key_block, query_pos, key_pos)
        weights = jnp.exp(scores - lse[:, :, None])
        d_probs = jnp.einsum(
            "rhe,khe->hrk", d_heads, value_block, preferred_element_type=jnp.float32
        )
        d_scores = (weights * (d_probs - delta[:, :, None])).astype(jnp.bfloat16)
        return summed + jnp.einsum(
            "hrk,khe->rhe", d_scores, key_block, preferred_element_type=jnp.float32
        )

    summed = lax.fori_loop(
        0, block_count, advance, jnp.zeros((row_count, head_count, HEAD), jnp.float32)
    )
    return (summed * HEAD ** (-0.5)).reshape(row_count, head_count * HEAD).astype(jnp.bfloat16)


def shards_by_rows(queries, key_rows, value_rows, gate_in, gate_out, kernel_taps, norm_gain, cotangent):
    row_count = queries.shape[0]
    channels = queries.shape[1]
    head_count = channels // HEAD
    group_count = kernel_taps.shape[0]
    devices = lax.axis_size("ctx")
    position = lax.axis_index("ctx")
    own_first = position * row_count
    total_rows = row_count * devices
    block_rows = min(512, total_rows)
    local_pos = jnp.arange(row_count, dtype=jnp.int32)
    keys_all, values_all = (
        lax.all_gather(key_rows, "ctx", axis=0, tiled=True),
        lax.all_gather(value_rows, "ctx", axis=0, tiled=True),
    )
    keys_heads = keys_all.reshape(total_rows, head_count, HEAD)
    query_sets = (queries, own_first + local_pos)
    query_block, query_pos = query_sets
    block_count = query_pos[-1] // block_rows + 1
    lse_sets = row_totals(
        query_block.reshape(-1, head_count, HEAD), query_pos, block_count, keys_heads, block_rows
    )
    values_heads = values_all.reshape(total_rows, head_count, HEAD)
    query_block, query_pos = query_sets
    outputs = row_outputs(
        query_block.reshape(-1, head_count, HEAD),
        query_pos,
        block_count,
        keys_heads,
        values_heads,
        lse_sets,
        block_rows,
    )
    lse_rows = lse_sets.T
    attn_wide = outputs.astype(jnp.float32)
    square_sum = lax.psum(jnp.sum(attn_wide * attn_wide, axis=1), "chan")
    inverse_rms = 1.0 / jnp.sqrt(square_sum / WIDTH + EPS)
    normed = attn_wide * inverse_rms[:, None] * norm_gain[None, :]
    gate_wide = gate_in.astype(jnp.float32)
    mixed_in = gate_wide * normed
    taps = jnp.broadcast_to(
        kernel_taps[:, None, :], (group_count, channels // group_count, FILT)
    ).reshape(channels, FILT)
    rim_before = from_behind(mixed_in[row_count - (FILT - 1) :], "ctx", 1)
    extended = jnp.concatenate([rim_before, mixed_in], axis=0)
    conv_out = jnp.zeros((row_count, channels), jnp.float32)
    for lag in range(FILT):
        conv_out = (
            conv_out + taps[:, lag][None, :] * extended[FILT - 1 - lag : FILT - 1 - lag + row_count]
        )
    out_gate = gate_out.astype(jnp.float32)
    mixed = (out_gate * conv_out).astype(jnp.bfloat16)
    upstream = cotangent.astype(jnp.float32)
    grad_gate_out = (upstream * conv_out).astype(jnp.bfloat16)
    d_conv = upstream * out_gate
    tap_columns = []
    for lag in range(FILT):
        per_channel = jnp.sum(
            d_conv * extended[FILT - 1 - lag : FILT - 1 - lag + row_count], axis=0
        )
        tap_columns.append(per_channel.reshape(group_count, -1).sum(axis=1))
    tap_terms = jnp.stack(tap_columns, axis=1)
    rim_after = from_behind(d_conv[: FILT - 1], "ctx", -1)
    extended_grad = jnp.concatenate([d_conv, rim_after], axis=0)
    d_mixed = jnp.zeros((row_count, channels), jnp.float32)
    for lag in range(FILT):
        d_mixed = d_mixed + taps[:, lag][None, :] * extended_grad[lag : lag + row_count]
    grad_gate_in = (d_mixed * normed).astype(jnp.bfloat16)
    d_normed = d_mixed * gate_wide
    gain_terms = jnp.sum(d_normed * attn_wide * inverse_rms[:, None], axis=0)
    grad_filter, grad_gain = lax.psum((tap_terms, gain_terms), "ctx")
    scaled = d_normed * norm_gain[None, :]
    row_dot = lax.psum(jnp.sum(scaled * attn_wide, axis=1), "chan")
    d_attn = (
        inverse_rms[:, None] * scaled - attn_wide * (inverse_rms**3 * row_dot / WIDTH)[:, None]
    ).astype(jnp.bfloat16)
    d_heads = d_attn.reshape(row_count, head_count, HEAD)
    delta_rows = jnp.sum(
        d_heads.astype(jnp.float32) * attn_wide.reshape(row_count, head_count, HEAD), axis=2
    )
    own_count = (own_first + row_count - 1) // block_rows + 1
    grad_queries = query_grads(
        queries.reshape(row_count, head_count, HEAD),
        d_heads,
        own_first + local_pos,
        own_count,
        keys_heads,
        values_heads,
        lse_rows.T,
        delta_rows.T,
        block_rows,
    )
    lse_all, delta_all = (
        lax.all_gather(lse_rows, "ctx", axis=0, tiled=True),
        lax.all_gather(delta_rows, "ctx", axis=0, tiled=True),
    )
    own_keys = key_rows.reshape(row_count, head_count, HEAD)
    own_values = value_rows.reshape(row_count, head_count, HEAD)
    key_pos = own_first + local_pos
    empty_grad = jnp.zeros((row_count, head_count, HEAD), jnp.float32)
    query_piece = lax.all_gather(queries, "ctx", axis=0, tiled=True)
    d_piece = lax.all_gather(d_attn, "ctx", axis=0, tiled=True)
    piece_rows = query_piece.shape[0]

    def contribute(totals):
        query_heads = query_piece.reshape(piece_rows, head_count, HEAD)
        piece_heads = d_piece.reshape(piece_rows, head_count, HEAD)
        query_pos = jnp.arange(piece_rows, dtype=jnp.int32)
        lse_piece = lse_all.T
        delta_piece = delta_all.T
        scores = score_block(query_heads, own_keys, query_pos, key_pos)
        weights = jnp.exp(scores - lse_piece[:, :, None])
        d_probs = jnp.einsum(
            "rhe,khe->hrk", piece_heads, own_values, preferred_element_type=jnp.float32
        )
        d_scores = (weights * (d_probs - delta_piece[:, :, None])).astype(jnp.bfloat16)
        key_grad = jnp.einsum(
            "hrk,rhe->khe", d_scores, query_heads, preferred_element_type=jnp.float32
        )
        value_grad = jnp.einsum(
            "hrk,rhe->khe",
            weights.astype(jnp.bfloat16),
            piece_heads,
            preferred_element_type=jnp.float32,
        )
        return (key_grad, value_grad)

    def unchanged(totals):
        return totals

    key_grad, value_grad = lax.cond(
        jnp.int32(0) + piece_rows > own_first, contribute, unchanged, (empty_grad, empty_grad)
    )
    grad_keys = (key_grad * HEAD ** (-0.5)).reshape(row_count, channels).astype(jnp.bfloat16)
    grad_values = value_grad.reshape(row_count, channels).astype(jnp.bfloat16)
    return (
        mixed,
        grad_queries,
        grad_keys,
        grad_values,
        grad_gate_in,
        grad_gate_out,
        grad_filter,
        grad_gain,
    )


LOG2E = 1.4426950408889634
VMEM_LIMIT = 14 * 1024 * 1024
PACK_LIMIT = 54400 * 1024


def vmem_call(body, ins, outs, scratch=(), limit=VMEM_LIMIT, flags=None, **extra):
    return pl.pallas_call(
        body,
        in_specs=ins,
        out_specs=tuple(spec for spec, _ in outs),
        out_shape=tuple(shape for _, shape in outs),
        scratch_shapes=list(scratch),
        compiler_params=pltpu.CompilerParams(vmem_limit_bytes=limit, flags=flags),
        **extra,
    )


def step(size, at):
    return [*range(0, size, 2), *range(1, size, 2)][at]


def set_apart(size):
    return range(size - size // 2 + 1, size)


def target(axis, at):
    size = lax.axis_size(axis)
    return lax.rem(lax.axis_index(axis) + step(size, at), size)


def origin(axis, at):
    size = lax.axis_size(axis)
    return lax.rem(lax.axis_index(axis) + size - step(size, at), size)


def start_all(copies):
    copies = list(copies)
    for copy in copies:
        copy.start()
    return copies


def wait_all(copies):
    for copy in copies:
        copy.wait()


def arrive(axis, pieces, held, tail=False):
    count = held.shape[1]
    for s, piece in enumerate(pieces):
        first = piece.shape[0] - count if tail else 0
        held[origin(axis, s)] = piece[first : first + count, :]


def depart(axis, held, pieces):
    for s, piece in enumerate(pieces):
        piece[...] = held[target(axis, s)]


def shift(piece, axis, by):
    size = lax.axis_size(axis)
    return lax.ppermute(piece, axis, [(i, (i + step(size, by)) % size) for i in range(size)])


def exchange(pieces, axis):
    size = lax.axis_size(axis)
    return [pieces[0]] + [shift(pieces[s], axis, s) for s in range(1, size)]


def dot_nt(a, b, precision=None):
    return lax.dot_general(
        a, b, (((1,), (1,)), ((), ())), precision=precision, preferred_element_type=jnp.float32
    )


def dot_nn(a, b):
    return lax.dot_general(a, b, (((1,), (0,)), ((), ())), preferred_element_type=jnp.float32)


def row_sums_as_lanes(product):
    ones = jnp.ones((8, product.shape[1]), jnp.bfloat16)
    high = product.astype(jnp.bfloat16)
    rest = (product - high.astype(jnp.float32)).astype(jnp.bfloat16)
    return (dot_nt(ones, high) + dot_nt(ones, rest))[0:1]


def channel_taps(taps_ref, head):
    groups = taps_ref.shape[1]
    size = HEAD * lax.axis_size("ctx") // groups
    wanted = head * (HEAD // size) + lax.broadcasted_iota(jnp.int32, (groups, HEAD), 1) // size
    spread = (wanted == lax.broadcasted_iota(jnp.int32, (groups, HEAD), 0)).astype(jnp.float32)
    return lax.dot_general(
        taps_ref[...],
        spread,
        (((1,), (0,)), ((), ())),
        precision=lax.Precision.HIGHEST,
        preferred_element_type=jnp.float32,
    )


def pack_body(axis, *refs):
    blocks = lax.axis_size(axis)
    arrays, refs = refs[:6], refs[6:]
    outs, apart, bufs, sems = refs[:blocks], refs[blocks:-7], refs[-7:-1], refs[-1]
    rows = arrays[0].shape[0]
    coming = start_all(
        pltpu.make_async_copy(ref, buf, sems.at[at]) for at, (ref, buf) in enumerate(zip(arrays, bufs))
    )
    gates = dict(zip(set_apart(blocks), apart))

    def store(at, s, block):
        if at >= 3 and s in gates:
            gates[s][(at - 3) * rows : (at - 2) * rows, :] = block
        else:
            outs[s][at * rows : (at + 1) * rows, :] = block

    columns = [pl.ds(pl.multiple_of(target(axis, s) * HEAD, HEAD), HEAD) for s in range(blocks)]
    for at in range(4):
        coming[at].wait()
        for s in range(blocks):
            store(at, s, bufs[at][:, columns[s]])
    wait_all(coming[4:])
    for s in range(blocks):
        d_conv = bufs[4][:, columns[s]].astype(jnp.float32) * bufs[5][:, columns[s]].astype(jnp.float32)
        store(4, s, d_conv.astype(jnp.bfloat16))


def coefficient_body(axis, token_ref, taps_ref, gain_ref, coef_ref):
    mine = lax.axis_index(axis)
    coef_ref[0:FILT, :] = channel_taps(taps_ref, mine)
    coef_ref[FILT : FILT + 1, :] = gain_ref[pl.ds(mine, 1), :]


def prepare_body(axis, token_ref, taps_ref, go_ref, ct_ref, wide_ref, dz_ref, du_pad):
    heads = lax.axis_size(axis)
    rows = go_ref.shape[0]
    du_pad[rows : rows + 8, :] = jnp.zeros((8, du_pad.shape[1]), jnp.float32)
    du_pad[0:rows, :] = go_ref[...].astype(jnp.float32) * ct_ref[...].astype(jnp.float32)
    for head in range(heads):
        cols = slice(head * HEAD, (head + 1) * HEAD)
        taps = channel_taps(taps_ref, head)
        wide_ref[0:FILT, cols] = taps
        dz = jnp.zeros((rows, HEAD), jnp.float32)
        for lag in range(FILT):
            dz = dz + taps[lag : lag + 1, :] * du_pad[lag : lag + rows, cols]
        dz_ref[:, cols] = dz


def attend_body(axis, *refs):
    blocks = lax.axis_size(axis)
    pieces, (p_ref, attn_ref, sq_ref, rx_ref) = refs[:blocks], refs[blocks:]
    arrive(axis, pieces, rx_ref)
    rows = rx_ref.shape[1] // 3
    tokens = blocks * rows
    wide = 2 * rows if blocks % 2 == 0 else rows
    per = wide // rows

    def part(at, first, count):
        return rx_ref[first : first + count, at * rows : (at + 1) * rows, :].reshape(count * rows, HEAD)

    v_t = part(2, 0, blocks).astype(jnp.float32).T.astype(jnp.bfloat16)
    scale = HEAD ** (-0.5) * LOG2E
    for i in range(tokens // wide):
        first, keys = i * wide, (i + 1) * wide
        s = dot_nt(part(1, 0, (i + 1) * per), part(0, i * per, per))
        key_pos = lax.broadcasted_iota(jnp.int32, (wide, wide), 0)
        query_pos = lax.broadcasted_iota(jnp.int32, (wide, wide), 1)
        edge = jnp.where(key_pos <= query_pos, s[first:], NEG)
        s = edge if i == 0 else jnp.concatenate([s[:first], edge], axis=0)
        top = jnp.max(s, axis=0, keepdims=True)
        e = jnp.exp2((s - top) * scale)
        p = (e * (1.0 / jnp.sum(e, axis=0, keepdims=True))).astype(jnp.bfloat16)
        p_ref[:keys, first:keys] = p
        attn_t = dot_nn(v_t[:, :keys], p).astype(jnp.bfloat16).astype(jnp.float32)
        squares = jnp.sum(attn_t * attn_t, axis=0, keepdims=True)
        for j in range(per):
            sq_ref[i * per + j : i * per + j + 1, :] = squares[:, j * rows : (j + 1) * rows]
        attn_ref[first:keys, :] = attn_t.T.astype(jnp.bfloat16)


def rowdot_body(axis, *refs):
    blocks = lax.axis_size(axis)
    pieces, refs = refs[:blocks], refs[blocks:]
    coef_ref, attn_ref, sq_ref, dz_ref, pay_ref, du_pad, sums, gate_ref = refs
    arrive(axis, pieces, gate_ref, tail=True)
    rows = gate_ref.shape[1] // 2
    tokens = blocks * rows
    for b in range(blocks):
        du_pad[b * rows : (b + 1) * rows, :] = gate_ref[b, rows:, :].astype(jnp.float32)
    du_pad[tokens : tokens + 8, :] = jnp.zeros((8, HEAD), jnp.float32)
    for b in range(blocks):
        first = b * rows
        dz = jnp.zeros((rows, HEAD), jnp.float32)
        for lag in range(FILT):
            dz = dz + coef_ref[lag : lag + 1, :] * du_pad[first + lag : first + lag + rows, :]
        dz_ref[first : first + rows, :] = dz
        scaled = dz * gate_ref[b, :rows, :].astype(jnp.float32) * coef_ref[FILT : FILT + 1, :]
        attn = attn_ref[first : first + rows, :].astype(jnp.float32)
        sums[blocks + b : blocks + b + 1, :] = row_sums_as_lanes(scaled * attn)
    sums[0:blocks, :] = sq_ref[...]
    low = sums[...].astype(jnp.bfloat16)
    for d in range(pay_ref.shape[0]):
        pay_ref[d] = low


def backward_body(axis, width, *refs):
    blocks = lax.axis_size(axis)
    pieces, gate_pieces, refs = refs[:blocks], refs[blocks : 2 * blocks], refs[2 * blocks :]
    rs_ref, coef_ref, p_ref, attn_ref, dz_ref = refs[:5]
    outs, (z_pad, ds_ref, da_ref, dl_ref, rx_ref, gate_ref, out_ref) = refs[5 : 5 + blocks], refs[5 + blocks :]
    arrive(axis, pieces, rx_ref)
    arrive(axis, gate_pieces, gate_ref, tail=True)
    rows = gate_ref.shape[1] // 2
    tokens = blocks * rows
    wide = 2 * rows if blocks % 2 == 0 else rows
    per = wide // rows
    gain = coef_ref[FILT : FILT + 1, :]

    def part(at, first, count):
        return rx_ref[first : first + count, at * rows : (at + 1) * rows, :].reshape(count * rows, HEAD)

    totals = jnp.sum(rs_ref[...].astype(jnp.float32), axis=0)
    rstd_lanes = 1.0 / jnp.sqrt(totals[:blocks] / width + EPS)
    pull_lanes = rstd_lanes * rstd_lanes * rstd_lanes * totals[blocks:] / width
    z_pad[0:8, :] = jnp.zeros((8, HEAD), jnp.float32)
    grads = [jnp.zeros((1, HEAD), jnp.float32) for _ in range(FILT + 1)]
    for b in range(blocks):
        first = b * rows
        rstd = jnp.broadcast_to(rstd_lanes[b : b + 1], (HEAD, rows)).T
        pull = jnp.broadcast_to(pull_lanes[b : b + 1], (HEAD, rows)).T
        attn = attn_ref[first : first + rows, :].astype(jnp.float32)
        dz = dz_ref[first : first + rows, :]
        gi = gate_ref[b, :rows, :].astype(jnp.float32)
        du = gate_ref[b, rows:, :].astype(jnp.float32)
        normed = attn * rstd * gain
        z_pad[8 + first : 8 + first + rows, :] = gi * normed
        for lag in range(FILT):
            z = z_pad[8 + first - lag : 8 + first - lag + rows, :]
            grads[lag] = grads[lag] + jnp.sum(du * z, axis=0, keepdims=True)
        out_ref[b, 3 * rows : 4 * rows, :] = normed.astype(jnp.bfloat16)
        edge = jnp.concatenate([z_pad[first : first + 8, :], dz[rows - 8 :]], axis=0)
        out_ref[b, 4 * rows : 4 * rows + 16, :] = edge.astype(jnp.bfloat16)
        d_normed = dz * gi
        grads[FILT] = grads[FILT] + jnp.sum(d_normed * attn * rstd, axis=0, keepdims=True)
        d_attn = (rstd * (d_normed * gain) - attn * pull).astype(jnp.bfloat16)
        da_ref[first : first + rows, :] = d_attn
        dl_ref[0:1, first : first + rows] = row_sums_as_lanes(d_attn.astype(jnp.float32) * attn)
    both = jnp.concatenate(grads, axis=0)
    high = both.astype(jnp.bfloat16).astype(jnp.float32)
    both = jnp.concatenate([high, both - high], axis=0).astype(jnp.bfloat16)
    for b in range(blocks):
        out_ref[b, 4 * rows + 16 : 4 * rows + 32, :] = both
    scale = HEAD ** (-0.5)
    k_t = part(1, 0, blocks).astype(jnp.float32).T.astype(jnp.bfloat16)
    for i in range(tokens // wide):
        first, keys = i * wide, (i + 1) * wide
        dp = dot_nt(part(2, 0, (i + 1) * per), da_ref[first : first + wide, :])
        p = p_ref[:keys, first : first + wide].astype(jnp.float32)
        ds = (p * (dp - dl_ref[0:1, first : first + wide])).astype(jnp.bfloat16)
        ds_ref[:keys, first : first + wide] = ds
        gq = (dot_nn(k_t[:, :keys], ds) * scale).T.astype(jnp.bfloat16)
        for j in range(per):
            out_ref[i * per + j, 0:rows, :] = gq[j * rows : (j + 1) * rows]
    for i in range(tokens // wide):
        first = i * wide
        q = part(0, i * per, blocks - i * per)
        gk = (dot_nn(ds_ref[first : first + wide, first:], q) * scale).astype(jnp.bfloat16)
        gv = dot_nn(p_ref[first : first + wide, first:], da_ref[first:, :]).astype(jnp.bfloat16)
        for j in range(per):
            out_ref[i * per + j, rows : 2 * rows, :] = gk[j * rows : (j + 1) * rows]
            out_ref[i * per + j, 2 * rows : 3 * rows, :] = gv[j * rows : (j + 1) * rows]
    depart(axis, out_ref, outs)


def gate_blocks(axis, s, piece, gi_ref, go_ref, ct_ref, dz_ref, wide_ref, z_pad):
    rows = gi_ref.shape[0]
    cols = pl.ds(pl.multiple_of(origin(axis, s) * HEAD, HEAD), HEAD)
    edge = piece[4 * rows : 4 * rows + 16, :].astype(jnp.float32)
    normed = piece[3 * rows : 4 * rows, :].astype(jnp.float32)
    z_pad[s, 0:8, :] = edge[0:8]
    z_pad[s, 8 : 8 + rows, :] = gi_ref[:, cols].astype(jnp.float32) * normed
    dz = jnp.concatenate([dz_ref[0 : rows - 8, cols], edge[8:16]], axis=0)
    conv = jnp.zeros((rows, HEAD), jnp.float32)
    for lag in range(FILT):
        conv = conv + wide_ref[lag : lag + 1, cols] * z_pad[s, 8 - lag : 8 - lag + rows, :]
    return (
        (dz * normed).astype(jnp.bfloat16),
        (go_ref[:, cols].astype(jnp.float32) * conv).astype(jnp.bfloat16),
        (ct_ref[:, cols].astype(jnp.float32) * conv).astype(jnp.bfloat16),
    )


def sooner_body(axis, count, *refs):
    pieces, inputs, (out_ref, z_pad) = refs[:count], refs[count : count + 5], refs[count + 5 :]
    for s, piece in enumerate(pieces):
        for at, block in enumerate(gate_blocks(axis, s, piece, *inputs, z_pad)):
            out_ref[s, at] = block


def unpack_body(axis, *refs):
    heads = lax.axis_size(axis)
    pieces, refs = refs[:heads], refs[heads:]
    inputs, sooner_ref = refs[:5], refs[5]
    outs, (gf_ref, gg_ref), bufs, (z_pad, sems) = refs[6:12], refs[12:14], refs[14:20], refs[20:]
    rows = inputs[0].shape[0]
    leaving = [
        pltpu.make_async_copy(buf, ref, sems.at[at]) for at, (buf, ref) in enumerate(zip(bufs, outs))
    ]
    columns = [pl.ds(pl.multiple_of(origin(axis, s) * HEAD, HEAD), HEAD) for s in range(heads)]
    for at in range(3):
        for s, piece in enumerate(pieces):
            bufs[at][:, columns[s]] = piece[at * rows : (at + 1) * rows, :]
        leaving[at].start()
    for s, piece in enumerate(pieces):
        if s < sooner_ref.shape[0]:
            blocks = [sooner_ref[s, at] for at in range(3)]
        else:
            blocks = gate_blocks(axis, s, piece, *inputs, z_pad)
        for at, block in enumerate(blocks):
            bufs[3 + at][:, columns[s]] = block
    for at in range(3, 6):
        leaving[at].start()
    groups = gf_ref.shape[1]
    size = HEAD * heads // groups
    channel = lax.broadcasted_iota(jnp.int32, (HEAD, groups), 0)
    group = lax.broadcasted_iota(jnp.int32, (HEAD, groups), 1)
    totals = jnp.zeros((16, groups), jnp.float32)
    for s, piece in enumerate(pieces):
        head = origin(axis, s)
        both = piece[4 * rows + 16 : 4 * rows + 32, :]
        gather = (head * (HEAD // size) + channel // size == group).astype(jnp.bfloat16)
        totals = totals + dot_nn(both, gather)
        total = both.astype(jnp.float32)
        gg_ref[pl.ds(head, 1), :] = total[FILT : FILT + 1] + total[8 + FILT : 8 + FILT + 1]
    gf_ref[...] = totals[:FILT] + totals[8 : 8 + FILT]
    wait_all(leaving)


def cost(flops, moved):
    return pl.CostEstimate(flops=flops, bytes_accessed=moved, transcendentals=0)


def shards_by_heads(
    queries, key_rows, value_rows, gate_in, gate_out, kernel_taps, norm_gain, cotangent
):
    rows, channels = queries.shape
    heads = channels // HEAD
    tokens = rows * heads
    everyone = lax.axis_size("ctx") * lax.axis_size("chan")
    low, full = jnp.bfloat16, jnp.float32
    near, far = pl.BlockSpec(memory_space=pltpu.VMEM), pl.BlockSpec(memory_space=pl.ANY)
    hbm = pl.BlockSpec(memory_space=pltpu.HBM)

    def here(shape, dtype):
        return near, jax.ShapeDtypeStruct(shape, dtype)

    def there(shape, dtype):
        return far, jax.ShapeDtypeStruct(shape, dtype)

    gain = norm_gain.reshape(heads, HEAD)
    taps = kernel_taps.T
    apart = set_apart(heads)
    flat = pltpu.VMEM((rows, channels), low)
    width = channels * lax.axis_size("chan")
    packed = vmem_call(
        functools.partial(pack_body, "ctx"),
        [hbm] * 6,
        [here(((3 if s in apart else 5) * rows, HEAD), low) for s in range(heads)]
        + [here((2 * rows, HEAD), low)] * len(apart),
        [flat] * 6 + [pltpu.SemaphoreType.DMA((6,))],
        limit=PACK_LIMIT,
    )(queries, key_rows, value_rows, gate_in, gate_out, cotangent)
    qkv = exchange(packed[:heads], "ctx")
    gates = list(qkv)
    for s, piece in zip(apart, packed[heads:]):
        gates[s] = shift(piece, "ctx", s)
    (coef,) = vmem_call(
        functools.partial(coefficient_body, "ctx"),
        [far] + [near] * 2,
        [here((8, HEAD), full)],
        cost_estimate=cost(rows * channels, rows * channels),
    )(packed[0], taps, gain)
    probs, attn, squares = vmem_call(
        functools.partial(attend_body, "ctx"),
        [near] * heads,
        [here((tokens, tokens), low), here((tokens, HEAD), low), here((heads, rows), full)],
        [pltpu.VMEM((heads, 3 * rows, HEAD), low)],
        cost_estimate=cost(4 * tokens * tokens * HEAD, 16 * tokens * tokens),
    )(*qkv)
    d_mixed, partial = vmem_call(
        functools.partial(rowdot_body, "ctx"),
        [near] * (heads + 3),
        [here((tokens, HEAD), full), here((everyone, 2 * heads, rows), low)],
        [
            pltpu.VMEM((tokens + 8, HEAD), full),
            pltpu.VMEM((2 * heads, rows), full),
            pltpu.VMEM((heads, 2 * rows, HEAD), low),
        ],
        cost_estimate=cost(rows * channels, rows * channels),
    )(*gates, coef, attn, squares)
    sums = lax.all_to_all(partial, ("ctx", "chan"), 0, 0, tiled=True)
    grads = vmem_call(
        functools.partial(backward_body, "ctx", width),
        [near] * (2 * heads + 5),
        [here((4 * rows + 32, HEAD), low)] * heads,
        [
            pltpu.VMEM((tokens + 8, HEAD), full),
            pltpu.VMEM((tokens, tokens), low),
            pltpu.VMEM((tokens, HEAD), low),
            pltpu.VMEM((8, tokens), full),
            pltpu.VMEM((heads, 3 * rows, HEAD), low),
            pltpu.VMEM((heads, 2 * rows, HEAD), low),
            pltpu.VMEM((heads, 4 * rows + 32, HEAD), low),
        ],
    )(*qkv, *gates, sums, coef, probs, attn, d_mixed)
    wide, own_d_mixed = vmem_call(
        functools.partial(prepare_body, "ctx"),
        [far] + [near] * 3,
        [here((8, channels), full), here((rows, channels), full)],
        [pltpu.VMEM((rows + 8, channels), full)],
        cost_estimate=cost(rows * channels * 20, rows * channels * 32),
    )(grads[0], taps, gate_out, cotangent)
    back = exchange(grads, "ctx")
    count = heads // 2
    token_side = (gate_in, gate_out, cotangent, own_d_mixed, wide)
    padded = pltpu.VMEM((heads, rows + 8, HEAD), full)
    (sooner,) = vmem_call(
        functools.partial(sooner_body, "ctx", count),
        [near] * (count + 5),
        [here((count, 3, rows, HEAD), low)],
        [padded],
        cost_estimate=cost(rows * channels * 20, rows * channels * 16),
    )(*back[:count], *token_side)
    spread = (hbm, jax.ShapeDtypeStruct((rows, channels), low))
    gq, gk, gv, ggi, mixed, ggo, gf, gg = vmem_call(
        functools.partial(unpack_body, "ctx"),
        [near] * (heads + 6),
        [spread] * 6 + [here(kernel_taps.shape[::-1], full), here((heads, HEAD), full)],
        [flat] * 6 + [padded, pltpu.SemaphoreType.DMA((6,))],
    )(*back, *token_side, sooner)
    return (mixed, gq, gk, gv, ggi, ggo, gf.T, gg.reshape(channels))


def shards(queries, *rest):
    rows, channels = queries.shape
    by_heads = channels // HEAD == lax.axis_size("ctx") and rows == HEAD
    return (shards_by_heads if by_heads else shards_by_rows)(queries, *rest)


def solution(mesh):
    placed = (
        P("ctx", "chan"),
        P("ctx", "chan"),
        P("ctx", "chan"),
        P("ctx", "chan"),
        P("ctx", "chan"),
        P("chan", None),
        P("chan"),
        P("ctx", "chan"),
    )
    return jax.shard_map(
        shards,
        mesh=mesh,
        in_specs=placed,
        out_specs=(
            P("ctx", "chan"),
            P("ctx", "chan"),
            P("ctx", "chan"),
            P("ctx", "chan"),
            P("ctx", "chan"),
            P("ctx", "chan"),
            P("chan", None),
            P("chan"),
        ),
        check_vma=False,
    )
```
